512 devices in a mesh: row: 8 (over z), col: 8 (over x, core), depth: 8 (over y).
Axes of the slice: x: 4, y: 8, z: 8, core: 2. Of those that a mesh axis runs over, the one named last changes fastest.
Arguments:
- x_matrix: bfloat16 [4608, 4608], P(('row', 'depth'), 'col'), may hold values from -0.09375 to 0.09375
- tangent: bfloat16 [4608, 4608], P(('row', 'depth'), 'col'), may hold values from -6 to 6
- fill_x: int32 [36, 36], replicated, may hold values from 0 to 1, as said below
- fill_t: int32 [36, 36], replicated, may hold values from 0 to 1, as said below
Outputs:
- tangent_next: float32 [4608, 4608], P(('row', 'depth'), 'col')
The draws below stay inside these ranges and needn't reach their ends.
Inputs may be any that keep to these rules, and one draw needn't show every extreme that they name: `fill_x`: 1 where the block of X is filled, else 0; every diagonal block is filled. `fill_t`: 1 where the block of X' is filled, else 0; every diagonal block is filled.
All inputs are finite; a program needn't handle non-finite values.
Results may differ from the reference program's by a relative error of at most 0.00098.
Values may be sent and summed in bfloat16 or wider, within the bound.
A program may use at most 64 MiB of HBM per device.

```python
import jax
import jax.numpy as jnp
from jax import lax

BLOCK = 128
MATRIX = 4608


def fill_pattern(key, salt):
    key = jax.random.fold_in(key, salt)
    level_key, pick_key = jax.random.split(key)
    count = (MATRIX + BLOCK - 1) // BLOCK
    levels = jax.random.randint(level_key, (count,), 1, 8)
    picks = jax.random.randint(pick_key, (count, count), 0, 8)
    index = lax.iota(jnp.int32, count)
    diagonal = index[:, None] == index[None, :]
    filled = (picks < levels[:, None]) | diagonal
    return filled.astype(jnp.int32)


def draw_fill_x(key, part):
    return fill_pattern(key, 11)


def draw_fill_t(key, part):
    return fill_pattern(key, 23)


def block_levels(key, shape, pieces, smallest, largest):
    def one(dim, blocks):
        steps = jax.random.uniform(jax.random.fold_in(jax.random.fold_in(key, 6), dim), (blocks,), jnp.float32, smallest / len(pieces), largest / len(pieces))
        return jnp.repeat(jnp.exp(steps), shape[dim] // blocks).reshape((-1,) + (1,) * (len(shape) - dim - 1))

    level = one(*pieces[0])
    for cut in pieces[1:]:
        level = level * one(*cut)
    return level


def scatter_about(key, extent, spread, bound, pieces=(), kind=jnp.bfloat16):
    result = spread * jax.random.normal(key, extent, jnp.float32)
    if pieces:
        result = result * block_levels(key, extent, pieces, -0.22, 0.18)
    return jnp.clip(result, -bound, bound).astype(kind)


def setup_inputs(seed: int = 0) -> dict:
    arg_keys = jax.random.split(jax.random.key(seed), 5)
    x_matrix = scatter_about(arg_keys[0], (MATRIX, MATRIX), MATRIX ** -0.5, 0.09375, ((0, 64), (1, 8)))
    tangent = scatter_about(arg_keys[1], (MATRIX, MATRIX), 1.0, 6.0, ((0, 64), (1, 8)))
    fill_x = draw_fill_x(jax.random.fold_in(arg_keys[4], 71), 0)
    fill_t = draw_fill_t(jax.random.fold_in(arg_keys[4], 71), 0)
    return {"x_matrix": x_matrix, "tangent": tangent, "fill_x": fill_x, "fill_t": fill_t}


def expand(fill):
    full = jnp.repeat(jnp.repeat(fill.astype(jnp.float32), BLOCK, axis=0), BLOCK, axis=1)
    return full[:MATRIX, :MATRIX]


def product(left, right):
    return jnp.dot(left, right, preferred_element_type=jnp.float32)


def reference(x_matrix, tangent, fill_x, fill_t):
    masked_x = (x_matrix.astype(jnp.float32) * expand(fill_x)).astype(jnp.bfloat16)
    masked_t = (tangent.astype(jnp.float32) * expand(fill_t)).astype(jnp.bfloat16)
    square = product(masked_x, masked_x).astype(jnp.bfloat16)
    cross = product(masked_t, masked_x).astype(jnp.bfloat16)
    total = product(masked_t, square) + product(masked_x, cross) + product(square, masked_t)
    return 1.5 * masked_t.astype(jnp.float32) - 0.5 * total
```

```python
import functools

import jax
import jax.numpy as jnp
from jax import lax
from jax.experimental import pallas as pl
from jax.experimental.pallas import tpu as pltpu
from jax.sharding import PartitionSpec as P

BLOCK = 128
MESH = pl.DeviceIdType.MESH
F32 = jnp.float32
BF16 = jnp.bfloat16
N = 8
NX = 4
ROWS = 72
PAD = 80
WIDTH = 576
LANES = 640
HALVES = ((0, 256), (256, 320))


def kernel(
    x_ref, t_ref, fx_ref, ft_ref, out_ref,
    a1_send, a1_recv, lt, left, ra0, ra1, rb0, rb1,
    p_s0, p_d0, p_f0, p_s1, p_d1, p_f1,
    y_s0, y_d0, y_f0, y_s1, y_d1, y_f1, tm,
    a1_ss, a1_rs, z_ss, z_rs, y_ss, y_rs, x_ss, x_rs, c_ss, c_rs,
):
    r = lax.axis_index("row")
    c = lax.axis_index("col")
    d = lax.axis_index("depth")
    chip = c // 2
    core = lax.rem(c, 2)

    def wrap(value, size):
        return lax.rem(value + 2 * size, size)

    def at_row(step):
        return (wrap(r + step, N), c, d)

    def at_depth(step):
        return (r, c, wrap(d + step, N))

    def at_chip(step):
        return (r, wrap(chip + step, NX) * 2 + core, d)

    partner = (r, chip * 2 + 1 - core, d)

    barrier = pltpu.get_barrier_semaphore()
    greeted = [at_row(1), at_row(-1), at_chip(1), at_chip(-1), partner]
    greeted += [at_depth(s) for s in range(1, N)]
    for device in greeted:
        pl.semaphore_signal(barrier, inc=1, device_id=device, device_id_type=MESH)

    row_start = (r * N + d) * ROWS
    col_start = c * WIDTH

    def expand(fill):
        count = fill.shape[0]
        row_ids = (row_start + lax.broadcasted_iota(jnp.int32, (ROWS, count), 0)) >> 7
        row_hot = (row_ids == lax.broadcasted_iota(jnp.int32, (ROWS, count), 1)).astype(F32)
        col_ids = (col_start + lax.broadcasted_iota(jnp.int32, (count, WIDTH), 1)) >> 7
        col_hot = (col_ids == lax.broadcasted_iota(jnp.int32, (count, WIDTH), 0)).astype(F32)
        inner = jnp.dot(row_hot, fill.astype(F32), preferred_element_type=F32)
        return jnp.dot(inner, col_hot, preferred_element_type=F32)

    rights_a = (ra0, ra1)
    rights_b = (rb0, rb1)
    parts = ((p_s0, p_d0, p_f0), (p_s1, p_d1, p_f1))
    slots = ((y_s0, y_d0, y_f0), (y_s1, y_d1, y_f1))

    def chunk(index):
        return pl.ds(pl.multiple_of(index * PAD, 16), PAD)

    def block(index):
        return pl.ds(pl.multiple_of(index * ROWS, 8), ROWS)

    for m, (ref, fill) in enumerate(((x_ref, fx_ref), (t_ref, ft_ref))):
        masked = ref[...].astype(F32) * expand(fill[...])
        if m == 1:
            tm[...] = masked
        tall = jnp.concatenate([masked, jnp.zeros((PAD - ROWS, WIDTH), F32)], axis=0)
        for j in range(N):
            piece = tall[:, j * ROWS : (j + 1) * ROWS]
            wide = jnp.concatenate([piece, jnp.zeros((PAD, 128 - ROWS), F32)], axis=1)
            a1_send[m, j] = wide.astype(BF16)
        for h, (start, width) in enumerate(HALVES):
            rights_a[h][m, chunk(r), :] = tall[:, start : start + width].astype(BF16)
    for m in range(2):
        a1_recv[m, d] = a1_send[m, d]

    pl.semaphore_wait(barrier, len(greeted))

    sent = []

    def copy(src, dst, send_sem, recv_sem, device):
        return pltpu.make_async_remote_copy(
            src_ref=src, dst_ref=dst, send_sem=send_sem, recv_sem=recv_sem,
            device_id=device, device_id_type=MESH,
        )

    def send(src, dst, send_sem, recv_sem, device):
        made = copy(src, dst, send_sem, recv_sem, device)
        made.start()
        sent.append(made)

    def a1_start(m):
        for s in (4, 3, 5, 2, 6, 1, 7):
            to = wrap(d + s, N)
            send(a1_send.at[m, to], a1_recv.at[m, d], a1_ss.at[m, s], a1_rs.at[m, s], (r, c, to))

    def a1_finish(m):
        for s in range(1, N):
            came = wrap(d - s, N)
            slot = a1_recv.at[m, came]
            copy(slot, slot, a1_ss.at[m, s], a1_rs.at[m, s], partner).wait_recv()
        stacked = a1_recv[m].astype(F32)[:, :ROWS, :].reshape(N * ROWS, 128)
        turned = jnp.transpose(stacked)[:ROWS]
        turned = jnp.concatenate([turned, jnp.zeros((PAD - ROWS, WIDTH), F32)], axis=0)
        turned = jnp.concatenate([turned, jnp.zeros((PAD, LANES - WIDTH), F32)], axis=1)
        lt[m, chunk(c), :] = turned.astype(BF16)

    x_steps = ((2, 1), (1, 2))

    def lt_chunk(m, owner_chip, owner_core):
        return lt.at[m, chunk(owner_chip * 2 + owner_core), :]

    def core_send(m, k, owner_chip):
        piece = lt_chunk(m, owner_chip, core)
        send(piece, piece, c_ss.at[m, k], c_rs.at[m, k], partner)

    def x_step(m, s):
        if s == 0:
            core_send(m, 0, chip)
        for e, sign in enumerate((1, -1)):
            steps = x_steps[m][e]
            owner = wrap(chip - sign * s, NX)
            piece = lt_chunk(m, owner, core)
            if 0 < s <= steps:
                copy(piece, piece, x_ss.at[m, e, s - 1], x_rs.at[m, e, s - 1], partner).wait_recv()
            if s < steps:
                send(piece, piece, x_ss.at[m, e, s], x_rs.at[m, e, s], at_chip(sign))
            if 0 < s <= steps:
                core_send(m, 1 + e if s == 1 else 3, owner)

    def left_finish(m):
        long = 1 if x_steps[m][0] == 2 else -1
        for k, owner in enumerate((chip, chip - 1, chip + 1, chip - 2 * long)):
            piece = lt_chunk(m, wrap(owner, NX), 1 - core)
            copy(piece, piece, c_ss.at[m, k], c_rs.at[m, k], partner).wait_recv()
        for i in range(LANES // 128):
            lanes = slice(i * 128, (i + 1) * 128)
            left[m, lanes, :] = jnp.transpose(lt[m, :, lanes].astype(F32)).astype(BF16)

    ring_steps = ((4, 3), (3, 4))

    def z_step(stage, h, m, s):
        buf = (rights_a, rights_b)[stage][h]
        u = stage * 4 + h * 2 + m
        for e, sign in enumerate((1, -1)):
            steps = ring_steps[m][e]
            piece = buf.at[m, chunk(wrap(r - sign * s, N)), :]
            if 0 < s <= steps:
                copy(piece, piece, z_ss.at[u, e, s - 1], z_rs.at[u, e, s - 1], partner).wait_recv()
            if s < steps:
                send(piece, piece, z_ss.at[u, e, s], z_rs.at[u, e, s], at_row(sign))

    def y_step(h, k, s):
        part, slot = parts[h][k], slots[h][k]
        u = h * 3 + k
        for e, sign in enumerate((1, -1)):
            steps = ring_steps[(k + h) % 2][e]
            mine = part.at[block(wrap(d + sign * (steps - s), N)), :]
            if 0 < s <= steps:
                held = slot.at[e, s - 1]
                copy(held, held, y_ss.at[u, e, s - 1], y_rs.at[u, e, s - 1], partner).wait_recv()
                if s < steps:
                    slot[e, s - 1] = slot[e, s - 1] + mine[...]
            if s < steps:
                source = mine if s == 0 else slot.at[e, s - 1]
                send(source, slot.at[e, s], y_ss.at[u, e, s], y_rs.at[u, e, s], at_depth(sign))

    def y_total(h, k):
        part, slot = parts[h][k], slots[h][k]
        plus, minus = ring_steps[(k + h) % 2]
        return part[block(d), :] + slot[0, plus - 1] + slot[1, minus - 1]

    def multiply(out, terms):
        tile = 288

        def one(i, carry):
            rows = pl.ds(pl.multiple_of(i * tile, 16), tile)
            total = None
            for m, right in terms:
                term = jnp.dot(left[m, rows, :], right[...], preferred_element_type=F32)
                total = term if total is None else total + term
            out[rows, :] = total
            return carry

        lax.fori_loop(0, WIDTH // tile, one, 0)

    def firsts(h, k):
        right_x, right_t = rights_a[h].at[0], rights_a[h].at[1]
        if k == 0:
            multiply(parts[h][0], ((0, right_x),))
        else:
            multiply(parts[h][1], ((1, right_x), (0, right_t)))

    def second_start(h, k):
        total = y_total(h, k)
        tall = jnp.concatenate([total, jnp.zeros((PAD - ROWS, total.shape[1]), F32)], axis=0)
        rights_b[h][k, chunk(r), :] = tall.astype(BF16)
        z_step(1, h, k, 0)

    def seconds(h):
        multiply(parts[h][2], ((1, rights_b[h].at[0]), (0, rights_b[h].at[1])))

    def finish(h):
        start, width = HALVES[h]
        lanes = slice(start, start + width)
        out_ref[:, lanes] = 1.5 * tm[:, lanes] - 0.5 * y_total(h, 2)

    def z_all(stage, h, s):
        for m in range(2):
            z_step(stage, h, m, s)

    a1_start(0)
    z_all(0, 0, 0)
    a1_start(1)
    z_all(0, 1, 0)
    z_all(0, 0, 1)
    z_all(0, 1, 1)
    a1_finish(0)
    x_step(0, 0)
    z_all(0, 0, 2)
    a1_finish(1)
    x_step(1, 0)
    z_all(0, 1, 2)
    x_step(0, 1)
    z_all(0, 0, 3)
    x_step(0, 2)
    x_step(1, 1)
    z_step(0, 0, 0, 4)
    left_finish(0)
    firsts(0, 0)
    y_step(0, 0, 0)
    x_step(1, 2)
    z_all(0, 1, 3)
    z_step(0, 0, 1, 4)
    left_finish(1)
    firsts(0, 1)
    y_step(0, 1, 0)
    y_step(0, 0, 1)
    z_step(0, 1, 0, 4)
    firsts(1, 0)
    y_step(1, 0, 0)
    y_step(0, 1, 1)
    z_step(0, 1, 1, 4)
    firsts(1, 1)
    y_step(0, 0, 2)
    y_step(1, 1, 0)
    y_step(0, 1, 2)
    y_step(1, 0, 1)
    y_step(0, 0, 3)
    y_step(1, 1, 1)
    y_step(0, 1, 3)
    y_step(1, 0, 2)
    y_step(0, 0, 4)
    second_start(0, 0)
    y_step(1, 1, 2)
    y_step(0, 1, 4)
    second_start(0, 1)
    z_step(1, 0, 0, 1)
    y_step(1, 0, 3)
    z_step(1, 0, 1, 1)
    y_step(1, 1, 3)
    z_step(1, 0, 0, 2)
    z_step(1, 0, 1, 2)
    y_step(1, 0, 4)
    second_start(1, 0)
    z_step(1, 0, 0, 3)
    z_step(1, 0, 1, 3)
    y_step(1, 1, 4)
    second_start(1, 1)
    z_step(1, 0, 0, 4)
    z_step(1, 0, 1, 4)
    seconds(0)
    y_step(0, 2, 0)
    for s in range(1, 4):
        z_all(1, 1, s)
        y_step(0, 2, s)
    z_all(1, 1, 4)
    seconds(1)
    y_step(1, 2, 0)
    y_step(0, 2, 4)
    finish(0)
    for s in range(1, 5):
        y_step(1, 2, s)
    finish(1)
    for made in sent:
        made.wait_send()


def body(x_matrix, tangent, fill_x, fill_t):
    def partial_shapes(width):
        return [pltpu.VMEM((WIDTH, width), F32)] * 3

    def slot_shapes(width):
        return [pltpu.VMEM((2, 4, ROWS, width), F32)] * 3

    w0, w1 = HALVES[0][1], HALVES[1][1]
    vmem = pl.BlockSpec(memory_space=pltpu.VMEM)
    dma = pltpu.SemaphoreType.DMA
    return pl.pallas_call(
        kernel,
        out_shape=jax.ShapeDtypeStruct((ROWS, WIDTH), F32),
        in_specs=[vmem] * 4,
        out_specs=vmem,
        scratch_shapes=[
            pltpu.VMEM((2, N, PAD, 128), BF16),
            pltpu.VMEM((2, N, PAD, 128), BF16),
            pltpu.VMEM((2, N * PAD, LANES), BF16),
            pltpu.VMEM((2, LANES, N * PAD), BF16),
            pltpu.VMEM((2, N * PAD, w0), BF16),
            pltpu.VMEM((2, N * PAD, w1), BF16),
            pltpu.VMEM((2, N * PAD, w0), BF16),
            pltpu.VMEM((2, N * PAD, w1), BF16),
            *partial_shapes(w0), *partial_shapes(w1),
            *slot_shapes(w0), *slot_shapes(w1),
            pltpu.VMEM((ROWS, WIDTH), F32),
            dma((2, N)), dma((2, N)),
            dma((8, 2, 4)), dma((8, 2, 4)),
            dma((6, 2, 4)), dma((6, 2, 4)),
            dma((2, 2, 2)), dma((2, 2, 2)),
            dma((2, 4)), dma((2, 4)),
        ],
        compiler_params=pltpu.CompilerParams(
            collective_id=0, has_side_effects=True, vmem_limit_bytes=48 * 1024 * 1024
        ),
    )(x_matrix, tangent, fill_x, fill_t)


def solution(mesh):
    placed = (P(("row", "depth"), "col"), P(("row", "depth"), "col"), P(), P())
    return jax.shard_map(
        body, mesh=mesh, in_specs=placed, out_specs=P(("row", "depth"), "col"), check_vma=False
    )
```

```python
import jax
import jax.numpy as jnp
from jax import lax
from jax.experimental import pallas as pl
from jax.experimental.pallas import tpu as pltpu
from jax.sharding import PartitionSpec as P

MESH = pl.DeviceIdType.MESH
F32 = jnp.float32
BF16 = jnp.bfloat16
N = 8
NX = 4
ROWS = 72
PAD = 80
WIDTH = 576
LANES = 640
CHUNKS = ((0, 1, 0), (1, 1, 0), (2, 1, 0), (3, 1, 0), (4, 0, 1))
Z_TREES = ((3, 0), (3, 1), (4, 0), (4, 1))
Y_TREES = ((4, 2),)
RING_STEPS = ((4, 3), (3, 4))
ORDER = (
    ("prep", 0), ("z0", 0, 0, 0), ("a1", 0), ("prep", 1), ("z0", 1, 1, 0), ("z0", 0, 1, 0), ("a1", 1),
    ("z0", 1, 0, 0), ("z0", 0, 0, 1), ("z0", 1, 1, 1), ("a1f", 0), ("z0", 1, 0, 1), ("z0", 0, 1, 1),
    ("z0", 0, 0, 2), ("z0", 1, 1, 2), ("a1f", 1), ("z0", 1, 0, 2), ("x", 0, 3), ("z0", 0, 1, 2),
    ("z0", 0, 0, 3), ("x", 0, 1), ("z0", 1, 1, 3), ("x", 1, 2), ("x", 0, 2), ("z0", 1, 0, 3), ("x", 1, 3),
    ("left", 0), ("x", 1, 1), ("z0", 0, 1, 3), ("z0", 0, 0, 4), ("dot1", 2, 0), ("y", 2, 0, 1, 0),
    ("y", 2, 0, 0, 0), ("dot1", 1, 0), ("y", 1, 0, 1, 0), ("dot1", 0, 0), ("z0", 1, 1, 4),
    ("y", 0, 0, 0, 0), ("y", 1, 0, 0, 0), ("left", 1), ("y", 0, 0, 1, 0), ("dot1", 2, 1), ("y", 2, 1, 0, 0),
    ("y", 2, 1, 1, 0), ("dot1", 0, 1), ("dot1", 3, 0), ("y", 0, 1, 1, 0), ("y", 0, 1, 0, 0),
    ("y", 2, 0, 1, 1), ("y", 2, 0, 0, 1), ("dot1", 1, 1), ("y", 1, 0, 1, 1), ("y", 0, 0, 0, 1),
    ("y", 1, 1, 0, 0), ("y", 3, 0, 1, 0), ("y", 2, 1, 1, 1), ("y", 2, 1, 0, 1), ("dot1", 4, 1),
    ("dot1", 4, 0), ("y", 1, 0, 0, 1), ("y", 0, 1, 1, 1), ("y", 0, 0, 1, 1), ("y", 2, 0, 0, 2),
    ("y", 0, 0, 0, 2), ("y", 2, 0, 1, 2), ("y", 1, 1, 1, 0), ("y", 0, 1, 0, 1), ("y", 2, 1, 1, 2),
    ("y", 2, 1, 0, 2), ("y", 0, 1, 1, 2), ("y", 1, 1, 0, 1), ("y", 1, 0, 1, 2), ("y", 2, 0, 0, 3),
    ("y", 0, 0, 1, 2), ("dot1", 3, 1), ("y", 3, 0, 1, 1), ("y", 0, 0, 0, 3), ("y", 3, 0, 0, 0),
    ("y", 3, 1, 0, 0), ("y", 2, 0, 1, 3), ("y", 2, 1, 1, 3), ("y", 0, 1, 0, 2), ("y", 0, 1, 1, 3),
    ("y", 2, 0, 0, 4), ("sum", 2, 0), ("y", 1, 1, 1, 1), ("z1", 2, 0, 0, 0), ("y", 1, 0, 1, 3),
    ("y", 1, 1, 0, 2), ("y", 0, 0, 1, 3), ("y", 1, 0, 0, 2), ("y", 0, 0, 0, 4), ("y", 2, 1, 0, 3),
    ("sum", 0, 0), ("z1", 2, 0, 1, 0), ("z1", 0, 0, 0, 0), ("y", 3, 0, 1, 2), ("y", 3, 1, 1, 0),
    ("z1", 0, 0, 1, 0), ("y", 3, 0, 0, 1), ("y", 2, 1, 1, 4), ("sum", 2, 1), ("z1", 2, 1, 1, 0),
    ("z1", 2, 1, 0, 0), ("y", 3, 1, 0, 1), ("y", 0, 1, 1, 4), ("y", 0, 1, 0, 3), ("sum", 0, 1),
    ("z1", 0, 1, 1, 0), ("y", 4, 0, 0, 0), ("z1", 0, 1, 0, 0), ("z1", 2, 0, 0, 1), ("y", 1, 1, 1, 2),
    ("y", 4, 0, 1, 0), ("y", 1, 1, 0, 3), ("y", 4, 1, 0, 0), ("y", 4, 1, 1, 0), ("z1", 2, 0, 1, 1),
    ("y", 1, 0, 1, 4), ("y", 1, 0, 0, 3), ("sum", 1, 0), ("z1", 1, 0, 0, 0), ("z1", 0, 0, 0, 1),
    ("z1", 1, 0, 1, 0), ("y", 3, 0, 0, 2), ("z1", 0, 0, 1, 1), ("y", 3, 0, 1, 3), ("z1", 2, 1, 0, 1),
    ("y", 3, 1, 0, 2), ("y", 3, 1, 1, 1), ("z1", 2, 1, 1, 1), ("y", 4, 0, 0, 1), ("z1", 0, 1, 1, 1),
    ("z1", 0, 1, 0, 1), ("y", 1, 1, 1, 3), ("z1", 2, 0, 0, 2), ("y", 1, 1, 0, 4), ("sum", 1, 1),
    ("z1", 1, 1, 1, 0), ("z1", 1, 1, 0, 0), ("z1", 2, 0, 1, 2), ("y", 4, 1, 1, 1), ("y", 4, 0, 1, 1),
    ("z1", 1, 0, 0, 1), ("z1", 1, 0, 1, 1), ("z1", 0, 0, 0, 2), ("y", 3, 0, 0, 3), ("y", 3, 0, 1, 4),
    ("sum", 3, 0), ("y", 4, 1, 0, 1), ("zt", 3, 0, 0), ("y", 3, 1, 0, 3), ("y", 3, 1, 1, 2),
    ("z1", 0, 1, 0, 2), ("y", 4, 0, 0, 2), ("z1", 0, 1, 1, 2), ("z1", 1, 1, 1, 1), ("z1", 2, 1, 1, 2),
    ("y", 4, 1, 1, 2), ("z1", 1, 1, 0, 1), ("z1", 2, 0, 0, 3), ("z1", 1, 0, 0, 2), ("z1", 0, 0, 1, 2),
    ("y", 4, 1, 0, 2), ("z1", 2, 1, 0, 2), ("z1", 1, 0, 1, 2), ("y", 4, 0, 1, 2), ("y", 3, 1, 0, 4),
    ("y", 3, 1, 1, 3), ("sum", 3, 1), ("zt", 3, 1, 0), ("y", 4, 0, 0, 3), ("y", 4, 1, 1, 3),
    ("z1", 2, 0, 1, 3), ("z1", 0, 0, 0, 3), ("z1", 1, 1, 1, 2), ("z1", 2, 1, 1, 3), ("zt", 3, 0, 3),
    ("zt", 3, 0, 5), ("y", 4, 1, 0, 3), ("z1", 1, 1, 0, 2), ("z1", 0, 1, 1, 3), ("y", 4, 0, 1, 3),
    ("y", 4, 0, 0, 4), ("z1", 1, 0, 0, 3), ("z1", 1, 0, 1, 3), ("z1", 0, 1, 0, 3), ("sum", 4, 0),
    ("zt", 4, 0, 0), ("z1", 0, 0, 1, 3), ("y", 4, 1, 1, 4), ("z1", 2, 1, 0, 3), ("sum", 4, 1),
    ("z1", 2, 0, 0, 4), ("z1", 1, 1, 1, 3), ("zt", 3, 1, 3), ("z1", 2, 1, 1, 4), ("zt", 3, 1, 5),
    ("z1", 0, 0, 0, 4), ("zt", 4, 1, 0), ("dot2", 2), ("z1", 1, 1, 0, 3), ("z1", 0, 1, 1, 4), ("dot2", 0),
    ("z1", 1, 0, 0, 4), ("y", 2, 2, 1, 0), ("y", 0, 2, 1, 0), ("y", 0, 2, 0, 0), ("y", 2, 2, 0, 0),
    ("z1", 1, 1, 1, 4), ("dot2", 1), ("y", 1, 2, 0, 0), ("zt", 4, 0, 3), ("dot2", 3), ("y", 3, 2, 0, 0),
    ("y", 1, 2, 1, 0), ("y", 3, 2, 1, 0), ("y", 0, 2, 0, 1), ("zt", 4, 0, 5), ("y", 0, 2, 1, 1),
    ("zt", 4, 1, 5), ("y", 2, 2, 0, 1), ("zt", 4, 1, 3), ("y", 2, 2, 1, 1), ("y", 1, 2, 0, 1),
    ("y", 3, 2, 0, 1), ("y", 1, 2, 1, 1), ("y", 0, 2, 0, 2), ("y", 3, 2, 1, 1), ("y", 2, 2, 0, 2),
    ("y", 0, 2, 1, 2), ("dot2", 4), ("yt", 4, 2, 0), ("y", 3, 2, 0, 2), ("y", 1, 2, 1, 2),
    ("y", 3, 2, 1, 2), ("y", 2, 2, 1, 2), ("y", 1, 2, 0, 2), ("y", 0, 2, 1, 3), ("y", 0, 2, 0, 3),
    ("yt", 4, 2, 1), ("yt", 4, 2, 2), ("y", 2, 2, 0, 3), ("y", 1, 2, 1, 3), ("y", 3, 2, 1, 3),
    ("y", 1, 2, 0, 3), ("y", 2, 2, 1, 3), ("y", 3, 2, 0, 3), ("y", 0, 2, 0, 4), ("fin", 0),
    ("y", 2, 2, 0, 4), ("fin", 2), ("y", 1, 2, 1, 4), ("fin", 1), ("fin", 4), ("y", 3, 2, 1, 4), ("fin", 3),
)


def chunk_width(h):
    _, tiles, fold = CHUNKS[h]
    return tiles * 128 + fold * 64


def chunk_rows(h):
    _, tiles, fold = CHUNKS[h]
    return tiles * ROWS + fold * 40


def pack(value, h):
    _, tiles, fold = CHUNKS[h]
    rows = [value[:, t * 128 : (t + 1) * 128] for t in range(tiles)]
    if fold:
        last = value[:, tiles * 128 :]
        low = jnp.concatenate([last[40:], jnp.zeros((8, 64), F32)], axis=0)
        rows.append(jnp.concatenate([last[:40], low], axis=1))
    return rows[0] if len(rows) == 1 else jnp.concatenate(rows, axis=0)


def unpack(value, h):
    _, tiles, fold = CHUNKS[h]
    columns = [value[t * ROWS : (t + 1) * ROWS] for t in range(tiles)]
    if fold:
        last = value[tiles * ROWS :]
        columns.append(jnp.concatenate([last[:, :64], last[:32, 64:]], axis=0))
    return columns[0] if len(columns) == 1 else jnp.concatenate(columns, axis=1)


def kernel(x_hbm, t_hbm, fx_hbm, ft_hbm, out_ref, *scratch):
    scratch = list(scratch)
    ins = [scratch.pop(0) for _ in range(4)]
    a1_send, a1_recv, lt, left, tm, right0 = [scratch.pop(0) for _ in range(6)]
    rights = [scratch.pop(0) for _ in CHUNKS]
    parts = [scratch.pop(0) for _ in CHUNKS]
    slots = [scratch.pop(0) for _ in CHUNKS]
    in_s, a1_ss, a1_rs, x_ss, x_rs, c_rs, z0_ss, z0_rs, z_ss, z_rs, y_ss, y_rs = scratch

    r = lax.axis_index("row")
    c = lax.axis_index("col")
    d = lax.axis_index("depth")
    chip = c // 2
    core = lax.rem(c, 2)

    def wrap(value, size):
        return lax.rem(value + 2 * size, size)

    def at_row(step):
        return (wrap(r + step, N), c, d)

    def at_depth(step):
        return (r, c, wrap(d + step, N))

    def at_chip(step):
        return (r, wrap(chip + step, NX) * 2 + core, d)

    partner = (r, chip * 2 + 1 - core, d)

    barrier = pltpu.get_barrier_semaphore()
    greeted = [at_depth(s) for s in (4, 3, 5, 2, 6, 1, 7)]
    greeted += [at_row(s) for s in ((1, -1, 3, -3) if Z_TREES else (1, -1))]
    greeted += [at_chip(1), at_chip(2), at_chip(3), partner]
    for device in greeted:
        pl.semaphore_signal(barrier, inc=1, device_id=device, device_id_type=MESH)

    fetches = [
        pltpu.make_async_copy(src, dst, in_s.at[k])
        for k, (src, dst) in enumerate(zip((x_hbm, t_hbm, fx_hbm, ft_hbm), ins))
    ]
    for k in (0, 2, 1, 3):
        fetches[k].start()

    row_start = (r * N + d) * ROWS
    col_start = c * WIDTH

    def expand(fill):
        count = fill.shape[0]
        row_ids = (row_start + lax.broadcasted_iota(jnp.int32, (ROWS, count), 0)) >> 7
        row_hot = (row_ids == lax.broadcasted_iota(jnp.int32, (ROWS, count), 1)).astype(F32)
        col_ids = (col_start + lax.broadcasted_iota(jnp.int32, (count, WIDTH), 1)) >> 7
        col_hot = (col_ids == lax.broadcasted_iota(jnp.int32, (count, WIDTH), 0)).astype(F32)
        inner = jnp.dot(row_hot, fill.astype(F32), preferred_element_type=F32)
        return jnp.dot(inner, col_hot, preferred_element_type=F32)

    def chunk(index):
        return pl.ds(pl.multiple_of(index * PAD, 16), PAD)

    def tall(value):
        return jnp.concatenate([value, jnp.zeros((PAD - ROWS, value.shape[1]), F32)], axis=0)

    def copy(src, dst, send_sem, recv_sem, device):
        return pltpu.make_async_remote_copy(
            src_ref=src, dst_ref=dst, send_sem=send_sem, recv_sem=recv_sem,
            device_id=device, device_id_type=MESH,
        )

    def send(src, dst, send_sem, recv_sem, device):
        copy(src, dst, send_sem, recv_sem, device).start()

    def received(piece, recv_sem):
        copy(piece, piece, recv_sem, recv_sem, partner).wait_recv()

    def all_sent(pieces, send_sem):
        copy(pieces, pieces, send_sem, send_sem, partner).wait_send()

    def prep(m):
        fetches[m].wait()
        fetches[2 + m].wait()
        masked = ins[m][...].astype(F32) * expand(ins[2 + m][...])
        if m == 1:
            tm[...] = masked
        padded = tall(masked)
        for j in range(N):
            piece = padded[:, j * ROWS : (j + 1) * ROWS]
            wide = jnp.concatenate([piece, jnp.zeros((PAD, 128 - ROWS), F32)], axis=1)
            a1_send[m, j] = wide.astype(BF16)
        right0[m, chunk(r), :] = padded.astype(BF16)
        a1_recv[m, d] = a1_send[m, d]
        if m == 0:
            pl.semaphore_wait(barrier, len(greeted))

    def a1(m):
        for s in (4, 3, 5, 2, 6, 1, 7):
            to = wrap(d + s, N)
            send(a1_send.at[m, to], a1_recv.at[m, d], a1_ss.at[m], a1_rs.at[m], (r, c, to))

    def lt_piece(m, owner_chip, owner_core):
        return lt.at[m, chunk(wrap(owner_chip, NX) * 2 + owner_core), :]

    def a1f(m):
        received(a1_recv.at[m, pl.ds(0, N - 1)], a1_rs.at[m])
        stacked = a1_recv[m].astype(F32)[:, :ROWS, :].reshape(N * ROWS, 128)
        turned = tall(jnp.transpose(stacked)[:ROWS])
        turned = jnp.concatenate([turned, jnp.zeros((PAD, LANES - WIDTH), F32)], axis=1)
        lt[m, chunk(c), :] = turned.astype(BF16)
        piece = lt_piece(m, chip, core)
        for q in (2, 1, 3):
            send(piece, piece, x_ss.at[m], x_rs.at[m, q - 1], at_chip(q))
        send(piece, piece, x_ss.at[m], c_rs.at[m], partner)

    def x(m, q):
        piece = lt_piece(m, chip - q, core)
        received(piece, x_rs.at[m, q - 1])
        send(piece, piece, x_ss.at[m], c_rs.at[m], partner)

    def left_panel(m):
        received(lt.at[m, pl.ds(0, NX * PAD), :], c_rs.at[m])
        for i in range(LANES // 128):
            lanes = slice(i * 128, (i + 1) * 128)
            left[m, lanes, :] = jnp.transpose(lt[m, :, lanes].astype(F32)).astype(BF16)

    def ring(buf, send_sem, recv_sems, m, e, s):
        sign, steps = (1, -1)[e], RING_STEPS[m][e]
        at = e * RING_STEPS[m][0]
        piece = buf.at[m, chunk(wrap(r - sign * s, N)), :]
        if s > 0:
            received(piece, recv_sems.at[at + s - 1])
        if s < steps:
            send(piece, piece, send_sem, recv_sems.at[at + s], at_row(sign))

    def z0(m, e, s):
        ring(right0, z0_ss.at[m], z0_rs.at[m], m, e, s)

    def z1(h, m, e, s):
        ring(rights[h], z_ss.at[h, m], z_rs.at[h, m], m, e, s)

    def zt(h, m, q):
        piece = rights[h].at[m, chunk(wrap(r - q, N)), :]
        if q > 0:
            received(piece, z_rs.at[h, m, q - 1])
        for step in {0: (3, -3, 1, -1), 3: (1, -1), 5: (1,)}[q]:
            there = (q + step) % N
            send(piece, piece, z_ss.at[h, m], z_rs.at[h, m, there - 1], at_row(step))

    def y(h, k, e, s):
        sign, (plus, minus) = (1, -1)[e], RING_STEPS[(k + h) % 2]
        steps = (plus, minus)[e]
        part, slot, at = parts[h], slots[h], 7 * k + e * plus
        dest = wrap(d + sign * (steps - s), N)
        if s > 0:
            received(slot.at[at + s - 1], y_rs.at[h, at + s - 1])
            if s < steps:
                slot[at + s - 1] = slot[at + s - 1] + part[k, dest]
        if s < steps:
            source = part.at[k, dest] if s == 0 else slot.at[at + s - 1]
            send(source, slot.at[at + s], y_ss.at[h], y_rs.at[h, at + s], at_depth(sign))

    def yt(h, k, stage):
        part, slot, at = parts[h], slots[h], 7 * k

        def go(source, index, step):
            send(source, slot.at[at + index], y_ss.at[h], y_rs.at[h, at + index], at_depth(step))

        def mine(step):
            return wrap(d + step, N)

        if stage == 0:
            for index, (away, step) in enumerate(((4, 1), (2, -1), (-2, 1), (1, 1), (-1, -1))):
                go(part.at[k, mine(away)], index, step)
        elif stage == 1:
            for index in (0, 1):
                received(slot.at[at + index], y_rs.at[h, at + index])
            slot[at] = slot[at] + slot[at + 1] + part[k, mine(3)]
            go(slot.at[at], 5, 3)
        else:
            received(slot.at[at + 2], y_rs.at[h, at + 2])
            slot[at + 2] = slot[at + 2] + part[k, mine(-3)]
            go(slot.at[at + 2], 6, -3)

    def y_total(h, k):
        at = 7 * k
        if (h, k) in Y_TREES:
            last = (3, 4, 5, 6)
            for index in last:
                received(slots[h].at[at + index], y_rs.at[h, at + index])
        else:
            last = (RING_STEPS[(k + h) % 2][0] - 1, 6)
        total = parts[h][k, d]
        for index in last:
            total = total + slots[h][at + index]
        return unpack(total, h)

    def multiply(h, k, terms):
        blocks = 4
        tile = blocks * ROWS

        def one(i, carry):
            rows = pl.ds(pl.multiple_of(i * tile, 16), tile)
            total = None
            for m, right in terms:
                term = jnp.dot(left[m, rows, :], right[...], preferred_element_type=F32)
                total = term if total is None else total + term
            for b in range(blocks):
                parts[h][k, i * blocks + b] = pack(total[b * ROWS : (b + 1) * ROWS], h)
            return carry

        lax.fori_loop(0, N // blocks, one, 0)

    def lanes_of(h):
        start = CHUNKS[h][0] * 128
        return slice(start, start + chunk_width(h))

    def dot1(h, k):
        right_x, right_t = (right0.at[m, :, lanes_of(h)] for m in range(2))
        multiply(h, k, ((0, right_x),) if k == 0 else ((1, right_x), (0, right_t)))

    def sum1(h, k):
        rights[h][k, chunk(r), :] = tall(y_total(h, k)).astype(BF16)

    def dot2(h):
        for m in range(2):
            if (h, m) in Z_TREES:
                for q in (1, 2, 4, 6, 7):
                    piece = rights[h].at[m, chunk(wrap(r - q, N)), :]
                    received(piece, z_rs.at[h, m, q - 1])
        multiply(h, 2, ((1, rights[h].at[0]), (0, rights[h].at[1])))

    def fin(h):
        lanes = lanes_of(h)
        out_ref[:, lanes] = 1.5 * tm[:, lanes] - 0.5 * y_total(h, 2)

    steps = {
        "prep": prep, "a1": a1, "a1f": a1f, "x": x, "left": left_panel, "z0": z0, "z1": z1, "zt": zt,
        "y": y, "yt": yt, "dot1": dot1, "sum": sum1, "dot2": dot2, "fin": fin,
    }
    for name, *which in ORDER:
        steps[name](*which)

    for m in range(2):
        all_sent(a1_send.at[m, pl.ds(0, N - 1)], a1_ss.at[m])
        all_sent(lt.at[m, pl.ds(0, 7 * PAD), :], x_ss.at[m])
        all_sent(right0.at[m, pl.ds(0, 7 * PAD), :], z0_ss.at[m])
        for h in range(len(CHUNKS)):
            all_sent(rights[h].at[m, pl.ds(0, 7 * PAD), :], z_ss.at[h, m])
    for h in range(len(CHUNKS)):
        all_sent(slots[h], y_ss.at[h])


def body(x_matrix, tangent, fill_x, fill_t):
    count = len(CHUNKS)
    vmem = pltpu.VMEM
    dma = pltpu.SemaphoreType.DMA
    hbm = pl.BlockSpec(memory_space=pl.ANY)
    return pl.pallas_call(
        kernel,
        out_shape=jax.ShapeDtypeStruct((ROWS, WIDTH), F32),
        in_specs=[hbm] * 4,
        out_specs=pl.BlockSpec(memory_space=vmem),
        scratch_shapes=[
            *[vmem(a.shape, a.dtype) for a in (x_matrix, tangent, fill_x, fill_t)],
            vmem((2, N, PAD, 128), BF16),
            vmem((2, N, PAD, 128), BF16),
            vmem((2, N * PAD, LANES), BF16),
            vmem((2, LANES, N * PAD), BF16),
            vmem((ROWS, WIDTH), F32),
            vmem((2, N * PAD, WIDTH), BF16),
            *[vmem((2, N * PAD, chunk_width(h)), BF16) for h in range(count)],
            *[vmem((3, N, chunk_rows(h), 128), F32) for h in range(count)],
            *[vmem((3 * 7, chunk_rows(h), 128), F32) for h in range(count)],
            dma((4,)),
            dma((2,)), dma((2,)),
            dma((2,)), dma((2, 3)), dma((2,)),
            dma((2,)), dma((2, 7)),
            dma((count, 2)), dma((count, 2, 7)),
            dma((count,)), dma((count, 3 * 7)),
        ],
        compiler_params=pltpu.CompilerParams(
            collective_id=0, has_side_effects=True, vmem_limit_bytes=60 * 1024 * 1024
        ),
    )(x_matrix, tangent, fill_x, fill_t)


def solution(mesh):
    placed = (P(("row", "depth"), "col"), P(("row", "depth"), "col"), P(), P())
    return jax.shard_map(
        body, mesh=mesh, in_specs=placed, out_specs=P(("row", "depth"), "col"), check_vma=False
    )
```

```python
import jax
import jax.numpy as jnp
from jax import lax
from jax.experimental import pallas as pl
from jax.experimental.pallas import tpu as pltpu
from jax.sharding import PartitionSpec as P

MESH = pl.DeviceIdType.MESH
F32 = jnp.float32
BF16 = jnp.bfloat16
N = 8
NX = 4
ROWS = 72
PAD = 80
WIDTH = 576
LANES = 640
CHUNKS = ((0, 1, 0), (1, 1, 0), (2, 1, 0), (3, 1, 0), (4, 0, 1))
Z_TREES = ((3, 0), (3, 1), (4, 0), (4, 1))
Y_TREES = ((4, 2),)
RING_STEPS = ((4, 3), (3, 4))
SHORT = 2
ORDER = (
    ("prep", 0), ("a1", 0), ("prep", 1), ("z0", 1, 1, 0), ("z0", 2, 0, 0), ("z0", 0, 0, 0), ("a1", 1),
    ("z0", 0, 1, 0), ("z0", 1, 0, 0), ("z0", 2, 0, 1), ("z0", 1, 1, 1), ("z0", 2, 1, 0), ("z0", 0, 0, 1),
    ("z0", 2, 0, 2), ("a1f", 0), ("z0", 1, 0, 1), ("z0", 0, 1, 1), ("z0", 1, 1, 2), ("z0", 2, 1, 1),
    ("z0", 0, 0, 2), ("a1f", 1), ("z0", 0, 1, 2), ("z0", 1, 0, 2), ("z0", 1, 1, 3), ("z0", 2, 0, 3),
    ("x", 0, 3), ("x", 0, 2), ("z0", 0, 0, 3), ("x", 0, 1), ("z0", 1, 0, 3), ("left", 0), ("x", 1, 2),
    ("z0", 2, 0, 4), ("x", 1, 1), ("z0", 1, 1, 4), ("dot1", 3, 0), ("y", 3, 0, 1, 0), ("y", 3, 0, 0, 0),
    ("dot1", 2, 0), ("x", 1, 3), ("z0", 0, 1, 3), ("y", 2, 0, 1, 0), ("y", 2, 0, 0, 0), ("z0", 0, 0, 4),
    ("dot1", 0, 0), ("dot1", 1, 0), ("y", 0, 0, 0, 0), ("y", 1, 0, 0, 0), ("y", 0, 0, 1, 0),
    ("y", 1, 0, 1, 0), ("left", 1), ("dot1", 0, 1), ("y", 0, 1, 0, 0), ("z0", 2, 1, 2), ("y", 0, 1, 1, 0),
    ("y", 3, 0, 0, 1), ("y", 3, 0, 1, 1), ("dot1", 3, 1), ("y", 2, 0, 0, 1), ("y", 3, 1, 0, 0),
    ("y", 2, 0, 1, 1), ("dot1", 1, 1), ("y", 0, 0, 1, 1), ("y", 1, 1, 1, 0), ("y", 0, 0, 0, 1),
    ("dot1", 2, 1), ("y", 1, 1, 0, 0), ("y", 0, 1, 1, 1), ("y", 2, 1, 0, 0), ("y", 0, 1, 0, 1),
    ("y", 2, 1, 1, 0), ("y", 3, 0, 1, 2), ("y", 1, 0, 0, 1), ("y", 1, 0, 1, 1), ("z0", 2, 1, 3),
    ("y", 2, 0, 1, 2), ("dot1", 4, 1), ("y", 2, 0, 0, 2), ("y", 0, 0, 0, 2), ("y", 0, 1, 1, 2),
    ("y", 2, 1, 1, 1), ("y", 0, 0, 1, 2), ("y", 3, 1, 1, 0), ("y", 1, 1, 0, 1), ("y", 0, 1, 0, 2),
    ("dot1", 4, 0), ("y", 3, 1, 0, 1), ("y", 1, 0, 1, 2), ("y", 3, 0, 0, 2), ("y", 2, 0, 0, 3),
    ("y", 1, 1, 1, 1), ("y", 0, 1, 1, 3), ("y", 0, 0, 0, 3), ("y", 2, 1, 1, 2), ("y", 2, 0, 1, 3),
    ("y", 2, 1, 0, 1), ("y", 1, 1, 0, 2), ("y", 3, 0, 1, 3), ("y", 4, 1, 1, 0), ("y", 4, 1, 0, 0),
    ("y", 3, 1, 0, 2), ("y", 4, 0, 0, 0), ("y", 3, 1, 1, 1), ("y", 1, 0, 0, 2), ("y", 1, 1, 1, 2),
    ("y", 2, 0, 0, 4), ("sum", 2, 0), ("z1", 2, 0, 0, 0), ("y", 0, 0, 1, 3), ("z1", 2, 0, 1, 0),
    ("y", 0, 1, 0, 3), ("y", 0, 1, 1, 4), ("sum", 0, 1), ("z1", 0, 1, 1, 0), ("y", 0, 0, 0, 4),
    ("z1", 0, 1, 0, 0), ("sum", 0, 0), ("y", 1, 0, 1, 3), ("z1", 0, 0, 1, 0), ("z1", 0, 0, 0, 0),
    ("y", 3, 0, 0, 3), ("y", 2, 1, 1, 3), ("y", 2, 1, 0, 2), ("y", 3, 0, 1, 4), ("sum", 3, 0),
    ("zt", 3, 0, 0), ("y", 1, 1, 0, 3), ("y", 4, 1, 1, 1), ("y", 3, 1, 1, 2), ("y", 3, 1, 0, 3),
    ("z1", 2, 0, 1, 1), ("z1", 2, 0, 0, 1), ("y", 4, 0, 1, 0), ("y", 1, 1, 1, 3), ("y", 4, 0, 0, 1),
    ("z1", 0, 1, 1, 1), ("y", 1, 0, 1, 4), ("z1", 0, 1, 0, 1), ("y", 1, 0, 0, 3), ("sum", 1, 0),
    ("z1", 0, 0, 0, 1), ("z1", 0, 0, 1, 1), ("y", 2, 1, 1, 4), ("y", 2, 1, 0, 3), ("z1", 1, 0, 0, 0),
    ("sum", 2, 1), ("z1", 2, 1, 1, 0), ("y", 1, 1, 0, 4), ("sum", 1, 1), ("z1", 2, 1, 0, 0),
    ("z1", 1, 1, 1, 0), ("y", 4, 1, 0, 1), ("z1", 1, 0, 1, 0), ("y", 4, 1, 1, 2), ("y", 3, 1, 1, 3),
    ("z1", 1, 1, 0, 0), ("y", 3, 1, 0, 4), ("sum", 3, 1), ("zt", 3, 1, 0), ("y", 4, 0, 1, 1),
    ("z1", 2, 0, 0, 2), ("y", 4, 0, 0, 2), ("z1", 0, 1, 1, 2), ("z1", 1, 0, 0, 1), ("z1", 2, 1, 1, 1),
    ("z1", 0, 0, 0, 2), ("z1", 2, 1, 0, 1), ("z1", 1, 1, 1, 1), ("y", 4, 0, 1, 2), ("z1", 0, 0, 1, 2),
    ("z1", 0, 1, 0, 2), ("z1", 1, 1, 0, 1), ("z1", 1, 0, 1, 1), ("zt", 3, 0, 3), ("y", 4, 1, 1, 3),
    ("y", 4, 1, 0, 2), ("y", 4, 0, 0, 3), ("zt", 3, 0, 5), ("z1", 2, 0, 1, 2), ("z1", 2, 0, 0, 3),
    ("z1", 0, 1, 1, 3), ("zt", 3, 1, 5), ("z1", 2, 1, 1, 2), ("z1", 1, 0, 0, 2), ("z1", 1, 1, 1, 2),
    ("zt", 3, 1, 3), ("z1", 0, 0, 0, 3), ("y", 4, 1, 0, 3), ("y", 4, 1, 1, 4), ("z1", 2, 1, 0, 2),
    ("z1", 1, 0, 1, 2), ("sum", 4, 1), ("z1", 0, 1, 0, 3), ("zt", 4, 1, 0), ("y", 4, 0, 0, 4),
    ("z1", 0, 0, 1, 3), ("z1", 2, 1, 1, 3), ("y", 4, 0, 1, 3), ("z1", 2, 0, 0, 4), ("z1", 1, 1, 0, 2),
    ("z1", 1, 1, 1, 3), ("sum", 4, 0), ("z1", 1, 0, 0, 3), ("z1", 0, 1, 1, 4), ("zt", 4, 0, 0), ("dot2", 3),
    ("y", 3, 2, 0, 0), ("z1", 2, 1, 0, 3), ("z1", 0, 0, 0, 4), ("dot2", 0), ("z1", 1, 0, 1, 3),
    ("y", 0, 2, 1, 0), ("y", 3, 2, 1, 0), ("y", 0, 2, 0, 0), ("z1", 2, 0, 1, 3), ("z1", 2, 1, 1, 4),
    ("dot2", 2), ("z1", 1, 1, 1, 4), ("y", 2, 2, 0, 0), ("y", 2, 2, 1, 0), ("zt", 4, 1, 3),
    ("z1", 1, 1, 0, 3), ("zt", 4, 1, 5), ("z1", 1, 0, 0, 4), ("dot2", 1), ("y", 1, 2, 1, 0),
    ("y", 3, 2, 0, 1), ("y", 0, 2, 1, 1), ("y", 1, 2, 0, 0), ("y", 0, 2, 0, 1), ("zt", 4, 0, 5),
    ("y", 3, 2, 1, 1), ("zt", 4, 0, 3), ("y", 2, 2, 0, 1), ("y", 2, 2, 1, 1), ("y", 3, 2, 0, 2),
    ("y", 1, 2, 1, 1), ("y", 0, 2, 1, 2), ("y", 1, 2, 0, 1), ("y", 3, 2, 1, 2), ("y", 0, 2, 0, 2),
    ("dot2", 4), ("yt", 4, 2, 0), ("y", 2, 2, 0, 2), ("y", 1, 2, 1, 2), ("y", 3, 2, 0, 3),
    ("y", 2, 2, 1, 2), ("y", 1, 2, 0, 2), ("y", 3, 2, 1, 3), ("yt", 4, 2, 1), ("y", 0, 2, 0, 3),
    ("yt", 4, 2, 2), ("y", 1, 2, 1, 3), ("y", 2, 2, 0, 3), ("y", 2, 2, 1, 3), ("y", 3, 2, 1, 4),
    ("y", 0, 2, 1, 3), ("y", 0, 2, 0, 4), ("fin", 0), ("fin", 3), ("y", 1, 2, 1, 4), ("y", 1, 2, 0, 3),
    ("fin", 1), ("y", 2, 2, 0, 4), ("fin", 2), ("fin", 4),
)


def chunk_width(h):
    _, tiles, fold = CHUNKS[h]
    return tiles * 128 + fold * 64


def chunk_rows(h):
    _, tiles, fold = CHUNKS[h]
    return tiles * ROWS + fold * 40


def pack(value, h):
    _, tiles, fold = CHUNKS[h]
    rows = [value[:, t * 128 : (t + 1) * 128] for t in range(tiles)]
    if fold:
        last = value[:, tiles * 128 :]
        low = jnp.concatenate([last[40:], jnp.zeros((8, 64), F32)], axis=0)
        rows.append(jnp.concatenate([last[:40], low], axis=1))
    return rows[0] if len(rows) == 1 else jnp.concatenate(rows, axis=0)


def unpack(value, h):
    _, tiles, fold = CHUNKS[h]
    columns = [value[t * ROWS : (t + 1) * ROWS] for t in range(tiles)]
    if fold:
        last = value[tiles * ROWS :]
        columns.append(jnp.concatenate([last[:, :64], last[:32, 64:]], axis=0))
    return columns[0] if len(columns) == 1 else jnp.concatenate(columns, axis=1)


def kernel(x_hbm, t_hbm, fx_hbm, ft_hbm, out_ref, *scratch):
    scratch = list(scratch)
    ins = [scratch.pop(0) for _ in range(4)]
    a1_send, a1_recv, lt, left, xm, tm, pairs, ends = [scratch.pop(0) for _ in range(8)]
    rights = [scratch.pop(0) for _ in CHUNKS]
    parts = [scratch.pop(0) for _ in CHUNKS]
    slots = [scratch.pop(0) for _ in CHUNKS]
    shorts = [scratch.pop(0) for _ in CHUNKS]
    in_s, a1_ss, a1_rs, x_ss, x_rs, c_rs, z0_ss, z0_rs, z_ss, z_rs, y_ss, y_rs, b_ss = scratch

    r = lax.axis_index("row")
    c = lax.axis_index("col")
    d = lax.axis_index("depth")
    chip = c // 2
    core = lax.rem(c, 2)

    def wrap(value, size):
        return lax.rem(value + 2 * size, size)

    def at_row(step):
        return (wrap(r + step, N), c, d)

    def at_depth(step):
        return (r, c, wrap(d + step, N))

    def at_chip(step):
        return (r, wrap(chip + step, NX) * 2 + core, d)

    partner = (r, chip * 2 + 1 - core, d)

    barrier = pltpu.get_barrier_semaphore()
    greeted = [at_depth(s) for s in (4, 3, 5, 2, 6, 1, 7)]
    greeted += [at_row(s) for s in ((1, -1, 3, -3) if Z_TREES else (1, -1))]
    greeted += [at_chip(1), at_chip(2), at_chip(3), partner]
    for device in greeted:
        pl.semaphore_signal(barrier, inc=1, device_id=device, device_id_type=MESH)

    fetches = [
        pltpu.make_async_copy(src, dst, in_s.at[k])
        for k, (src, dst) in enumerate(zip((x_hbm, t_hbm, fx_hbm, ft_hbm), ins))
    ]
    for k in (0, 2, 1, 3):
        fetches[k].start()

    row_start = (r * N + d) * ROWS
    col_start = c * WIDTH

    def expand(fill):
        count = fill.shape[0]
        row_ids = (row_start + lax.broadcasted_iota(jnp.int32, (ROWS, count), 0)) >> 7
        row_hot = (row_ids == lax.broadcasted_iota(jnp.int32, (ROWS, count), 1)).astype(F32)
        col_ids = (col_start + lax.broadcasted_iota(jnp.int32, (count, WIDTH), 1)) >> 7
        col_hot = (col_ids == lax.broadcasted_iota(jnp.int32, (count, WIDTH), 0)).astype(F32)
        inner = jnp.dot(row_hot, fill.astype(F32), preferred_element_type=F32)
        return jnp.dot(inner, col_hot, preferred_element_type=F32)

    def chunk(index):
        return pl.ds(pl.multiple_of(index * PAD, 16), PAD)

    def tall(value):
        return jnp.concatenate([value, jnp.zeros((PAD - ROWS, value.shape[1]), F32)], axis=0)

    def copy(src, dst, send_sem, recv_sem, device):
        return pltpu.make_async_remote_copy(
            src_ref=src, dst_ref=dst, send_sem=send_sem, recv_sem=recv_sem,
            device_id=device, device_id_type=MESH,
        )

    def send(src, dst, send_sem, recv_sem, device):
        copy(src, dst, send_sem, recv_sem, device).start()

    def received(piece, recv_sem):
        copy(piece, piece, recv_sem, recv_sem, partner).wait_recv()

    def all_sent(pieces, send_sem):
        copy(pieces, pieces, send_sem, send_sem, partner).wait_send()

    def prep(m):
        fetches[m].wait()
        fetches[2 + m].wait()
        masked = ins[m][...].astype(F32) * expand(ins[2 + m][...])
        (xm, tm)[m][...] = masked
        padded = tall(masked)
        for j in range(N):
            piece = padded[:, j * ROWS : (j + 1) * ROWS]
            wide = jnp.concatenate([piece, jnp.zeros((PAD, 128 - ROWS), F32)], axis=1)
            a1_send[m, j] = wide.astype(BF16)
        if m == 1:
            both = jnp.concatenate([xm[...], masked], axis=0)
            for u in range(2):
                pairs[u, r] = both[:, u * 256 : (u + 1) * 256].astype(BF16)
            last = jnp.concatenate([both[:ROWS, 512:], both[ROWS:, 512:]], axis=1)
            ends[r] = tall(last).astype(BF16)
        a1_recv[m, d] = a1_send[m, d]
        if m == 0:
            pl.semaphore_wait(barrier, len(greeted))

    def a1(m):
        for s in (4, 3, 5, 2, 6, 1, 7):
            to = wrap(d + s, N)
            send(a1_send.at[m, to], a1_recv.at[m, d], a1_ss.at[m], a1_rs.at[m], (r, c, to))

    def lt_piece(m, owner_chip, owner_core):
        return lt.at[m, chunk(wrap(owner_chip, NX) * 2 + owner_core), :]

    def a1f(m):
        received(a1_recv.at[m, pl.ds(0, N - 1)], a1_rs.at[m])
        stacked = a1_recv[m].astype(F32)[:, :ROWS, :].reshape(N * ROWS, 128)
        turned = tall(jnp.transpose(stacked)[:ROWS])
        turned = jnp.concatenate([turned, jnp.zeros((PAD, LANES - WIDTH), F32)], axis=1)
        lt[m, chunk(c), :] = turned.astype(BF16)
        piece = lt_piece(m, chip, core)
        for q in (2, 1, 3):
            send(piece, piece, x_ss.at[m], x_rs.at[m, q - 1], at_chip(q))
        send(piece, piece, x_ss.at[m], c_rs.at[m], partner)

    def x(m, q):
        piece = lt_piece(m, chip - q, core)
        received(piece, x_rs.at[m, q - 1])
        send(piece, piece, x_ss.at[m], c_rs.at[m], partner)

    def left_panel(m):
        received(lt.at[m, pl.ds(0, NX * PAD), :], c_rs.at[m])
        for i in range(LANES // 128):
            lanes = slice(i * 128, (i + 1) * 128)
            panel = lt[m, :, lanes].astype(F32)
            left[m, lanes, :] = jnp.transpose(panel).astype(BF16)
            if m == 0:
                split = panel.reshape(N, PAD, 128)
                moved = jnp.concatenate([split[:, ROWS:], split[:, :ROWS]], axis=1)
                left[2, lanes, :] = jnp.transpose(moved.reshape(N * PAD, 128)).astype(BF16)

    def ring(piece_of, send_sem, recv_sems, m, e, s):
        sign, steps = (1, -1)[e], RING_STEPS[m][e]
        at = e * RING_STEPS[m][0]
        piece = piece_of(wrap(r - sign * s, N))
        if s > 0:
            received(piece, recv_sems.at[at + s - 1])
        if s < steps:
            send(piece, piece, send_sem, recv_sems.at[at + s], at_row(sign))

    def z0(u, e, s):
        def piece_of(index):
            return ends.at[index] if u == 2 else pairs.at[u, index]

        ring(piece_of, z0_ss.at[u], z0_rs.at[u], u % 2, e, s)

    def z1(h, m, e, s):
        def piece_of(index):
            return rights[h].at[m, chunk(index), :]

        ring(piece_of, z_ss.at[h, m], z_rs.at[h, m], m, e, s)

    def zt(h, m, q):
        piece = rights[h].at[m, chunk(wrap(r - q, N)), :]
        if q > 0:
            received(piece, z_rs.at[h, m, q - 1])
        for step in {0: (3, -3, 1, -1), 3: (1, -1), 5: (1,)}[q]:
            there = (q + step) % N
            send(piece, piece, z_ss.at[h, m], z_rs.at[h, m, there - 1], at_row(step))

    def y(h, k, e, s):
        sign, (plus, minus) = (1, -1)[e], RING_STEPS[(k + h) % 2]
        steps = (plus, minus)[e]
        part, slot, at = parts[h], slots[h], 7 * k + e * plus
        dest = wrap(d + sign * (steps - s), N)
        short = SHORT if k == 1 else 0
        came = None
        if s > 0:
            piece = shorts[h].at[1, e, s - 1] if s <= short else slot.at[at + s - 1]
            received(piece, y_rs.at[h, at + s - 1])
            if s < steps:
                came = piece[...].astype(F32) + part[k, dest]
        if s == steps:
            return
        if s < short:
            value = part[k, dest] if came is None else came
            shorts[h][0, e, s] = value.astype(BF16)
            source, target, done = shorts[h].at[0, e, s], shorts[h].at[1, e, s], b_ss.at[h]
        else:
            source, target, done = part.at[k, dest], slot.at[at + s], y_ss.at[h]
            if came is not None:
                slot[at + s - 1] = came
                source = slot.at[at + s - 1]
        send(source, target, done, y_rs.at[h, at + s], at_depth(sign))

    def yt(h, k, stage):
        part, slot, at = parts[h], slots[h], 7 * k

        def go(source, index, step):
            send(source, slot.at[at + index], y_ss.at[h], y_rs.at[h, at + index], at_depth(step))

        def mine(step):
            return wrap(d + step, N)

        if stage == 0:
            for index, (away, step) in enumerate(((4, 1), (2, -1), (-2, 1), (1, 1), (-1, -1))):
                go(part.at[k, mine(away)], index, step)
        elif stage == 1:
            for index in (0, 1):
                received(slot.at[at + index], y_rs.at[h, at + index])
            slot[at] = slot[at] + slot[at + 1] + part[k, mine(3)]
            go(slot.at[at], 5, 3)
        else:
            received(slot.at[at + 2], y_rs.at[h, at + 2])
            slot[at + 2] = slot[at + 2] + part[k, mine(-3)]
            go(slot.at[at + 2], 6, -3)

    def y_total(h, k):
        at = 7 * k
        if (h, k) in Y_TREES:
            last = (3, 4, 5, 6)
            for index in last:
                received(slots[h].at[at + index], y_rs.at[h, at + index])
        else:
            last = (RING_STEPS[(k + h) % 2][0] - 1, 6)
        total = parts[h][k, d]
        for index in last:
            total = total + slots[h][at + index]
        return unpack(total, h)

    def multiply(h, k, terms):
        blocks = 4
        tile = blocks * ROWS

        def one(i, carry):
            rows = pl.ds(pl.multiple_of(i * tile, 16), tile)
            total = None
            for m, right in terms:
                term = jnp.dot(left[m, rows, :], right(), preferred_element_type=F32)
                total = term if total is None else total + term
            for b in range(blocks):
                parts[h][k, i * blocks + b] = pack(total[b * ROWS : (b + 1) * ROWS], h)
            return carry

        lax.fori_loop(0, N // blocks, one, 0)

    def lanes_of(h):
        start = CHUNKS[h][0] * 128
        return slice(start, start + chunk_width(h))

    def dot1(h, k):
        tile, tiles, _ = CHUNKS[h]

        def right(m):
            if tiles == 0:
                value = ends[:, :, m * 64 : (m + 1) * 64]
            else:
                at = (tile % 2) * 128
                value = pairs[tile // 2, :, m * 64 : m * 64 + PAD, at : at + 128]
            return value.reshape(N * PAD, value.shape[2])

        def right_x():
            return right(0)

        def right_t():
            return right(1)

        if k == 0:
            multiply(h, k, ((0, right_x),))
        else:
            multiply(h, k, ((1, right_x), (0 if tiles == 0 else 2, right_t)))

    def sum1(h, k):
        rights[h][k, chunk(r), :] = tall(y_total(h, k)).astype(BF16)

    def dot2(h):
        for m in range(2):
            if (h, m) in Z_TREES:
                for q in (1, 2, 4, 6, 7):
                    piece = rights[h].at[m, chunk(wrap(r - q, N)), :]
                    received(piece, z_rs.at[h, m, q - 1])
        multiply(h, 2, ((1, lambda: rights[h][0]), (0, lambda: rights[h][1])))

    def fin(h):
        lanes = lanes_of(h)
        out_ref[:, lanes] = 1.5 * tm[:, lanes] - 0.5 * y_total(h, 2)

    steps = {
        "prep": prep, "a1": a1, "a1f": a1f, "x": x, "left": left_panel, "z0": z0, "z1": z1, "zt": zt,
        "y": y, "yt": yt, "dot1": dot1, "sum": sum1, "dot2": dot2, "fin": fin,
    }
    for name, *which in ORDER:
        steps[name](*which)

    for m in range(2):
        all_sent(a1_send.at[m, pl.ds(0, N - 1)], a1_ss.at[m])
        all_sent(lt.at[m, pl.ds(0, 7 * PAD), :], x_ss.at[m])
        all_sent(pairs.at[m, pl.ds(0, N - 1)], z0_ss.at[m])
        for h in range(len(CHUNKS)):
            all_sent(rights[h].at[m, pl.ds(0, 7 * PAD), :], z_ss.at[h, m])
    all_sent(ends.at[pl.ds(0, N - 1)], z0_ss.at[2])
    for h in range(len(CHUNKS)):
        all_sent(slots[h].at[pl.ds(0, 3 * 7 - 2 * SHORT)], y_ss.at[h])
        all_sent(shorts[h].at[0], b_ss.at[h])


def body(x_matrix, tangent, fill_x, fill_t):
    count = len(CHUNKS)
    vmem = pltpu.VMEM
    dma = pltpu.SemaphoreType.DMA
    hbm = pl.BlockSpec(memory_space=pl.ANY)
    return pl.pallas_call(
        kernel,
        out_shape=jax.ShapeDtypeStruct((ROWS, WIDTH), F32),
        in_specs=[hbm] * 4,
        out_specs=pl.BlockSpec(memory_space=vmem),
        scratch_shapes=[
            *[vmem(a.shape, a.dtype) for a in (x_matrix, tangent, fill_x, fill_t)],
            vmem((2, N, PAD, 128), BF16),
            vmem((2, N, PAD, 128), BF16),
            vmem((2, N * PAD, LANES), BF16),
            vmem((3, LANES, N * PAD), BF16),
            vmem((ROWS, WIDTH), F32),
            vmem((ROWS, WIDTH), F32),
            vmem((2, N, 2 * ROWS, 256), BF16),
            vmem((N, PAD, 128), BF16),
            *[vmem((2, N * PAD, chunk_width(h)), BF16) for h in range(count)],
            *[vmem((3, N, chunk_rows(h), 128), F32) for h in range(count)],
            *[vmem((3 * 7, chunk_rows(h), 128), F32) for h in range(count)],
            *[vmem((2, 2, SHORT, chunk_rows(h), 128), BF16) for h in range(count)],
            dma((4,)),
            dma((2,)), dma((2,)),
            dma((2,)), dma((2, 3)), dma((2,)),
            dma((3,)), dma((3, 7)),
            dma((count, 2)), dma((count, 2, 7)),
            dma((count,)), dma((count, 3 * 7)), dma((count,)),
        ],
        compiler_params=pltpu.CompilerParams(
            collective_id=0, has_side_effects=True, vmem_limit_bytes=60 * 1024 * 1024
        ),
    )(x_matrix, tangent, fill_x, fill_t)


def solution(mesh):
    placed = (P(("row", "depth"), "col"), P(("row", "depth"), "col"), P(), P())
    return jax.shard_map(
        body, mesh=mesh, in_specs=placed, out_specs=P(("row", "depth"), "col"), check_vma=False
    )
```

```python
import jax
import jax.numpy as jnp
from jax import lax
from jax.experimental import pallas as pl
from jax.experimental.pallas import tpu as pltpu
from jax.sharding import PartitionSpec as P

MESH = pl.DeviceIdType.MESH
F32 = jnp.float32
BF16 = jnp.bfloat16
N = 8
NX = 4
ROWS = 72
PAD = 80
WIDTH = 576
LANES = 640
CHUNKS = ((0, 1, 0), (1, 1, 0), (2, 1, 0), (3, 1, 0), (4, 0, 1))
Z_TREES = ((3, 0), (3, 1), (4, 0), (4, 1))
Y_TREES = ((4, 2),)
RING_STEPS = ((4, 3), (3, 4))
ORDER = (
    ("prep", 0), ("a1", 0), ("prep", 1), ("z0", 2, 0, 0), ("z0", 1, 1, 0), ("a1", 1), ("z0", 0, 0, 0),
    ("z0", 0, 1, 0), ("z0", 2, 1, 0), ("z0", 1, 0, 0), ("z0", 2, 0, 1), ("z0", 1, 1, 1), ("z0", 0, 0, 1),
    ("z0", 0, 1, 1), ("a1f", 0), ("z0", 1, 0, 1), ("z0", 2, 0, 2), ("z0", 1, 1, 2), ("z0", 2, 1, 1),
    ("z0", 0, 0, 2), ("a1f", 1), ("z0", 1, 0, 2), ("z0", 0, 1, 2), ("x", 0, 3), ("z0", 1, 1, 3),
    ("z0", 2, 1, 2), ("z0", 0, 0, 3), ("x", 0, 2), ("z0", 2, 0, 3), ("z0", 1, 0, 3), ("x", 0, 1),
    ("z0", 0, 1, 3), ("left", 0), ("z0", 1, 1, 4), ("dot1", 2, 0), ("y", 2, 0, 1, 0), ("z0", 0, 0, 4),
    ("y", 2, 0, 0, 0), ("x", 1, 1), ("dot1", 1, 0), ("y", 1, 0, 1, 0), ("y", 1, 0, 0, 0), ("dot1", 0, 0),
    ("dot1", 3, 0), ("z0", 2, 1, 3), ("y", 0, 0, 1, 0), ("y", 3, 0, 1, 0), ("y", 0, 0, 0, 0), ("x", 1, 2),
    ("x", 1, 3), ("y", 3, 0, 0, 0), ("y", 2, 0, 1, 1), ("y", 2, 0, 0, 1), ("left", 1), ("y", 1, 0, 1, 1),
    ("y", 1, 0, 0, 1), ("dot1", 0, 1), ("y", 0, 1, 0, 0), ("y", 0, 0, 0, 1), ("y", 0, 1, 1, 0),
    ("dot1", 2, 1), ("y", 2, 1, 1, 0), ("y", 2, 1, 0, 0), ("y", 0, 0, 1, 1), ("dot1", 1, 1),
    ("y", 2, 0, 0, 2), ("y", 1, 1, 0, 0), ("y", 1, 0, 1, 2), ("y", 1, 1, 1, 0), ("dot1", 3, 1),
    ("y", 1, 0, 0, 2), ("y", 0, 1, 1, 1), ("y", 0, 0, 0, 2), ("y", 2, 1, 1, 1), ("y", 3, 1, 0, 0),
    ("y", 2, 0, 1, 2), ("z0", 2, 0, 4), ("y", 2, 0, 0, 3), ("y", 1, 0, 1, 3), ("y", 0, 0, 1, 2),
    ("dot1", 4, 0), ("y", 3, 1, 1, 0), ("y", 1, 1, 0, 1), ("y", 2, 1, 0, 1), ("y", 0, 0, 0, 3),
    ("dot1", 4, 1), ("y", 2, 1, 1, 2), ("y", 1, 0, 0, 3), ("y", 3, 1, 0, 1), ("y", 0, 1, 1, 2),
    ("y", 2, 0, 1, 3), ("y", 0, 1, 0, 1), ("y", 1, 0, 1, 4), ("sum", 1, 0), ("z1", 1, 0, 0, 0),
    ("y", 1, 1, 1, 1), ("y", 2, 0, 0, 4), ("z1", 1, 0, 1, 0), ("y", 3, 0, 1, 1), ("sum", 2, 0),
    ("y", 1, 1, 0, 2), ("y", 0, 0, 1, 3), ("y", 4, 0, 0, 0), ("z1", 2, 0, 1, 0), ("z1", 2, 0, 0, 0),
    ("y", 4, 0, 1, 0), ("y", 2, 1, 0, 2), ("y", 0, 0, 0, 4), ("sum", 0, 0), ("z1", 0, 0, 1, 0),
    ("y", 2, 1, 1, 3), ("z1", 0, 0, 0, 0), ("y", 3, 1, 1, 1), ("y", 3, 1, 0, 2), ("z1", 1, 0, 1, 1),
    ("z1", 1, 0, 0, 1), ("y", 0, 1, 1, 3), ("y", 0, 1, 0, 2), ("y", 1, 1, 1, 2), ("z1", 2, 0, 1, 1),
    ("z1", 2, 0, 0, 1), ("y", 1, 1, 0, 3), ("y", 3, 0, 0, 1), ("y", 3, 0, 1, 2), ("y", 2, 1, 0, 3),
    ("z1", 0, 0, 0, 1), ("y", 2, 1, 1, 4), ("sum", 2, 1), ("z1", 2, 1, 0, 0), ("z1", 2, 1, 1, 0),
    ("y", 4, 0, 0, 1), ("z1", 0, 0, 1, 1), ("y", 3, 1, 0, 3), ("y", 3, 1, 1, 2), ("z1", 1, 0, 0, 2),
    ("y", 0, 1, 0, 3), ("z1", 1, 0, 1, 2), ("y", 0, 1, 1, 4), ("sum", 0, 1), ("y", 4, 1, 1, 0),
    ("z1", 0, 1, 0, 0), ("z1", 2, 0, 0, 2), ("z1", 2, 0, 1, 2), ("y", 4, 1, 0, 0), ("z1", 0, 1, 1, 0),
    ("y", 1, 1, 1, 3), ("y", 1, 1, 0, 4), ("y", 4, 0, 1, 1), ("sum", 1, 1), ("z1", 1, 1, 0, 0),
    ("z1", 1, 1, 1, 0), ("z1", 0, 0, 0, 2), ("y", 3, 0, 0, 2), ("z1", 2, 1, 1, 1), ("y", 3, 0, 1, 3),
    ("z1", 2, 1, 0, 1), ("z1", 0, 0, 1, 2), ("y", 4, 0, 0, 2), ("z1", 1, 0, 0, 3), ("y", 3, 1, 0, 4),
    ("y", 3, 1, 1, 3), ("sum", 3, 1), ("zt", 3, 1, 0), ("y", 4, 1, 1, 1), ("z1", 1, 1, 1, 1),
    ("y", 4, 1, 0, 1), ("z1", 1, 0, 1, 3), ("z1", 0, 1, 1, 1), ("z1", 1, 1, 0, 1), ("z1", 0, 1, 0, 1),
    ("y", 4, 0, 1, 2), ("y", 3, 0, 1, 4), ("y", 3, 0, 0, 3), ("z1", 2, 1, 1, 2), ("sum", 3, 0),
    ("z1", 2, 0, 0, 3), ("y", 4, 0, 0, 3), ("z1", 2, 0, 1, 3), ("z1", 0, 0, 0, 3), ("z1", 1, 0, 0, 4),
    ("zt", 3, 0, 0), ("z1", 2, 1, 0, 2), ("y", 4, 1, 1, 2), ("z1", 1, 1, 1, 2), ("y", 4, 0, 1, 3),
    ("z1", 0, 1, 1, 2), ("z1", 1, 1, 0, 2), ("y", 4, 0, 0, 4), ("z1", 2, 1, 1, 3), ("z1", 0, 1, 0, 2),
    ("sum", 4, 0), ("y", 4, 1, 0, 2), ("zt", 4, 0, 0), ("y", 4, 1, 1, 3), ("z1", 1, 1, 1, 3),
    ("zt", 3, 1, 3), ("z1", 0, 1, 1, 3), ("zt", 3, 1, 5), ("zt", 3, 0, 5), ("z1", 2, 1, 1, 4),
    ("zt", 3, 0, 3), ("y", 4, 1, 0, 3), ("y", 4, 1, 1, 4), ("z1", 0, 0, 1, 3), ("z1", 2, 0, 0, 4),
    ("sum", 4, 1), ("zt", 4, 1, 0), ("z1", 1, 1, 0, 3), ("z1", 2, 1, 0, 3), ("dot2", 2), ("z1", 1, 1, 1, 4),
    ("z1", 0, 1, 0, 3), ("y", 2, 2, 0, 0), ("z1", 0, 0, 0, 4), ("y", 2, 2, 1, 0), ("dot2", 1),
    ("y", 1, 2, 1, 0), ("zt", 4, 0, 5), ("z1", 0, 1, 1, 4), ("y", 1, 2, 0, 0), ("dot2", 0),
    ("y", 0, 2, 1, 0), ("zt", 4, 0, 3), ("y", 0, 2, 0, 0), ("dot2", 3), ("y", 3, 2, 0, 0),
    ("y", 3, 2, 1, 0), ("y", 2, 2, 0, 1), ("y", 2, 2, 1, 1), ("zt", 4, 1, 5), ("zt", 4, 1, 3),
    ("y", 1, 2, 1, 1), ("y", 1, 2, 0, 1), ("y", 0, 2, 0, 1), ("y", 0, 2, 1, 1), ("y", 3, 2, 1, 1),
    ("y", 3, 2, 0, 1), ("y", 2, 2, 0, 2), ("y", 2, 2, 1, 2), ("dot2", 4), ("yt", 4, 2, 0),
    ("y", 0, 2, 0, 2), ("y", 1, 2, 1, 2), ("y", 3, 2, 1, 2), ("y", 1, 2, 0, 2), ("y", 0, 2, 1, 2),
    ("y", 2, 2, 1, 3), ("y", 2, 2, 0, 3), ("yt", 4, 2, 1), ("yt", 4, 2, 2), ("y", 1, 2, 1, 3),
    ("y", 0, 2, 0, 3), ("y", 3, 2, 0, 2), ("y", 1, 2, 0, 3), ("y", 3, 2, 1, 3), ("y", 0, 2, 1, 3),
    ("y", 0, 2, 0, 4), ("y", 2, 2, 0, 4), ("fin", 2), ("fin", 0), ("fin", 4), ("y", 1, 2, 1, 4), ("fin", 1),
    ("y", 3, 2, 1, 4), ("y", 3, 2, 0, 3), ("fin", 3),
)


def chunk_width(h):
    _, tiles, fold = CHUNKS[h]
    return tiles * 128 + fold * 64


def chunk_rows(h):
    _, tiles, fold = CHUNKS[h]
    return tiles * ROWS + fold * 40


def pack(value, h):
    _, tiles, fold = CHUNKS[h]
    rows = [value[:, t * 128 : (t + 1) * 128] for t in range(tiles)]
    if fold:
        last = value[:, tiles * 128 :]
        low = jnp.concatenate([last[40:], jnp.zeros((8, 64), F32)], axis=0)
        rows.append(jnp.concatenate([last[:40], low], axis=1))
    return rows[0] if len(rows) == 1 else jnp.concatenate(rows, axis=0)


def unpack(value, h):
    _, tiles, fold = CHUNKS[h]
    columns = [value[t * ROWS : (t + 1) * ROWS] for t in range(tiles)]
    if fold:
        last = value[tiles * ROWS :]
        columns.append(jnp.concatenate([last[:, :64], last[:32, 64:]], axis=0))
    return columns[0] if len(columns) == 1 else jnp.concatenate(columns, axis=1)


def kernel(x_hbm, t_hbm, fx_hbm, ft_hbm, out_ref, *scratch):
    scratch = list(scratch)
    ins = [scratch.pop(0) for _ in range(4)]
    a1_send, a1_recv, lt, left, xm, tm, pairs, ends = [scratch.pop(0) for _ in range(8)]
    rights = [scratch.pop(0) for _ in CHUNKS]
    parts = [scratch.pop(0) for _ in CHUNKS]
    slots = [scratch.pop(0) for _ in CHUNKS]
    in_s, a1_ss, a1_rs, x_ss, x_rs, c_rs, z0_ss, z0_rs, z_ss, z_rs, y_ss, y_rs = scratch

    r = lax.axis_index("row")
    c = lax.axis_index("col")
    d = lax.axis_index("depth")
    chip = c // 2
    core = lax.rem(c, 2)

    def wrap(value, size):
        return lax.rem(value + 2 * size, size)

    def at_row(step):
        return (wrap(r + step, N), c, d)

    def at_depth(step):
        return (r, c, wrap(d + step, N))

    def at_chip(step):
        return (r, wrap(chip + step, NX) * 2 + core, d)

    partner = (r, chip * 2 + 1 - core, d)

    barrier = pltpu.get_barrier_semaphore()
    greeted = [at_depth(s) for s in (4, 3, 5, 2, 6, 1, 7)]
    greeted += [at_row(s) for s in ((1, -1, 3, -3) if Z_TREES else (1, -1))]
    greeted += [at_chip(1), at_chip(2), at_chip(3), partner]
    for device in greeted:
        pl.semaphore_signal(barrier, inc=1, device_id=device, device_id_type=MESH)

    fetches = [
        pltpu.make_async_copy(src, dst, in_s.at[k])
        for k, (src, dst) in enumerate(zip((x_hbm, t_hbm, fx_hbm, ft_hbm), ins))
    ]
    for k in (0, 2, 1, 3):
        fetches[k].start()

    row_start = (r * N + d) * ROWS
    col_start = c * WIDTH

    def expand(fill):
        count = fill.shape[0]
        row_ids = (row_start + lax.broadcasted_iota(jnp.int32, (ROWS, count), 0)) >> 7
        row_hot = (row_ids == lax.broadcasted_iota(jnp.int32, (ROWS, count), 1)).astype(F32)
        col_ids = (col_start + lax.broadcasted_iota(jnp.int32, (count, WIDTH), 1)) >> 7
        col_hot = (col_ids == lax.broadcasted_iota(jnp.int32, (count, WIDTH), 0)).astype(F32)
        inner = jnp.dot(row_hot, fill.astype(F32), preferred_element_type=F32)
        return jnp.dot(inner, col_hot, preferred_element_type=F32)

    def chunk(index):
        return pl.ds(pl.multiple_of(index * PAD, 16), PAD)

    def tall(value):
        return jnp.concatenate([value, jnp.zeros((PAD - ROWS, value.shape[1]), F32)], axis=0)

    def copy(src, dst, send_sem, recv_sem, device):
        return pltpu.make_async_remote_copy(
            src_ref=src, dst_ref=dst, send_sem=send_sem, recv_sem=recv_sem,
            device_id=device, device_id_type=MESH,
        )

    def send(src, dst, send_sem, recv_sem, device):
        copy(src, dst, send_sem, recv_sem, device).start()

    def received(piece, recv_sem):
        copy(piece, piece, recv_sem, recv_sem, partner).wait_recv()

    def all_sent(pieces, send_sem):
        copy(pieces, pieces, send_sem, send_sem, partner).wait_send()

    def prep(m):
        fetches[m].wait()
        fetches[2 + m].wait()
        masked = ins[m][...].astype(F32) * expand(ins[2 + m][...])
        (xm, tm)[m][...] = masked
        padded = tall(masked)
        for j in range(N):
            piece = padded[:, j * ROWS : (j + 1) * ROWS]
            wide = jnp.concatenate([piece, jnp.zeros((PAD, 128 - ROWS), F32)], axis=1)
            a1_send[m, j] = wide.astype(BF16)
        if m == 1:
            both = jnp.concatenate([xm[...], masked], axis=0)
            for u in range(2):
                pairs[u, r] = both[:, u * 256 : (u + 1) * 256].astype(BF16)
            last = jnp.concatenate([both[:ROWS, 512:], both[ROWS:, 512:]], axis=1)
            ends[r] = tall(last).astype(BF16)
        a1_recv[m, d] = a1_send[m, d]
        if m == 0:
            pl.semaphore_wait(barrier, len(greeted))

    def a1(m):
        for s in (4, 3, 5, 2, 6, 1, 7):
            to = wrap(d + s, N)
            send(a1_send.at[m, to], a1_recv.at[m, d], a1_ss.at[m], a1_rs.at[m], (r, c, to))

    def lt_piece(m, owner_chip, owner_core):
        return lt.at[m, chunk(wrap(owner_chip, NX) * 2 + owner_core), :]

    def a1f(m):
        received(a1_recv.at[m, pl.ds(0, N - 1)], a1_rs.at[m])
        stacked = a1_recv[m].astype(F32)[:, :ROWS, :].reshape(N * ROWS, 128)
        turned = tall(jnp.transpose(stacked)[:ROWS])
        turned = jnp.concatenate([turned, jnp.zeros((PAD, LANES - WIDTH), F32)], axis=1)
        lt[m, chunk(c), :] = turned.astype(BF16)
        piece = lt_piece(m, chip, core)
        for q in (2, 1, 3):
            send(piece, piece, x_ss.at[m], x_rs.at[m, q - 1], at_chip(q))
        send(piece, piece, x_ss.at[m], c_rs.at[m], partner)

    def x(m, q):
        piece = lt_piece(m, chip - q, core)
        received(piece, x_rs.at[m, q - 1])
        send(piece, piece, x_ss.at[m], c_rs.at[m], partner)

    def left_panel(m):
        received(lt.at[m, pl.ds(0, NX * PAD), :], c_rs.at[m])
        for i in range(LANES // 128):
            lanes = slice(i * 128, (i + 1) * 128)
            panel = lt[m, :, lanes].astype(F32)
            left[m, lanes, :] = jnp.transpose(panel).astype(BF16)
            if m == 0:
                split = panel.reshape(N, PAD, 128)
                moved = jnp.concatenate([split[:, ROWS:], split[:, :ROWS]], axis=1)
                left[2, lanes, :] = jnp.transpose(moved.reshape(N * PAD, 128)).astype(BF16)

    def ring(piece_of, send_sem, recv_sems, m, e, s):
        sign, steps = (1, -1)[e], RING_STEPS[m][e]
        at = e * RING_STEPS[m][0]
        piece = piece_of(wrap(r - sign * s, N))
        if s > 0:
            received(piece, recv_sems.at[at + s - 1])
        if s < steps:
            send(piece, piece, send_sem, recv_sems.at[at + s], at_row(sign))

    def z0(u, e, s):
        def piece_of(index):
            return ends.at[index] if u == 2 else pairs.at[u, index]

        ring(piece_of, z0_ss.at[u], z0_rs.at[u], u % 2, e, s)

    def z1(h, m, e, s):
        def piece_of(index):
            return rights[h].at[m, chunk(index), :]

        ring(piece_of, z_ss.at[h, m], z_rs.at[h, m], m, e, s)

    def zt(h, m, q):
        piece = rights[h].at[m, chunk(wrap(r - q, N)), :]
        if q > 0:
            received(piece, z_rs.at[h, m, q - 1])
        for step in {0: (3, -3, 1, -1), 3: (1, -1), 5: (1,)}[q]:
            there = (q + step) % N
            send(piece, piece, z_ss.at[h, m], z_rs.at[h, m, there - 1], at_row(step))

    def y(h, k, e, s):
        sign, (plus, minus) = (1, -1)[e], RING_STEPS[(k + h) % 2]
        steps = (plus, minus)[e]
        part, slot, at = parts[h], slots[h], 7 * k + e * plus
        dest = wrap(d + sign * (steps - s), N)
        if s > 0:
            received(slot.at[at + s - 1], y_rs.at[h, at + s - 1])
            if s < steps:
                slot[at + s - 1] = slot[at + s - 1] + part[k, dest]
        if s < steps:
            source = part.at[k, dest] if s == 0 else slot.at[at + s - 1]
            send(source, slot.at[at + s], y_ss.at[h], y_rs.at[h, at + s], at_depth(sign))

    def yt(h, k, stage):
        part, slot, at = parts[h], slots[h], 7 * k

        def go(source, index, step):
            send(source, slot.at[at + index], y_ss.at[h], y_rs.at[h, at + index], at_depth(step))

        def mine(step):
            return wrap(d + step, N)

        if stage == 0:
            for index, (away, step) in enumerate(((4, 1), (2, -1), (-2, 1), (1, 1), (-1, -1))):
                go(part.at[k, mine(away)], index, step)
        elif stage == 1:
            for index in (0, 1):
                received(slot.at[at + index], y_rs.at[h, at + index])
            slot[at] = slot[at] + slot[at + 1] + part[k, mine(3)]
            go(slot.at[at], 5, 3)
        else:
            received(slot.at[at + 2], y_rs.at[h, at + 2])
            slot[at + 2] = slot[at + 2] + part[k, mine(-3)]
            go(slot.at[at + 2], 6, -3)

    def y_total(h, k):
        at = 7 * k
        if (h, k) in Y_TREES:
            last = (3, 4, 5, 6)
            for index in last:
                received(slots[h].at[at + index], y_rs.at[h, at + index])
        else:
            last = (RING_STEPS[(k + h) % 2][0] - 1, 6)
        total = parts[h][k, d]
        for index in last:
            total = total + slots[h][at + index]
        return unpack(total, h)

    def multiply(h, k, terms):
        blocks = 4
        tile = blocks * ROWS

        def one(i, carry):
            rows = pl.ds(pl.multiple_of(i * tile, 16), tile)
            total = None
            for m, right in terms:
                term = jnp.dot(left[m, rows, :], right(), preferred_element_type=F32)
                total = term if total is None else total + term
            for b in range(blocks):
                parts[h][k, i * blocks + b] = pack(total[b * ROWS : (b + 1) * ROWS], h)
            return carry

        lax.fori_loop(0, N // blocks, one, 0)

    def lanes_of(h):
        start = CHUNKS[h][0] * 128
        return slice(start, start + chunk_width(h))

    def dot1(h, k):
        tile, tiles, _ = CHUNKS[h]

        def right(m):
            if tiles == 0:
                value = ends[:, :, m * 64 : (m + 1) * 64]
            else:
                at = (tile % 2) * 128
                value = pairs[tile // 2, :, m * 64 : m * 64 + PAD, at : at + 128]
            return value.reshape(N * PAD, value.shape[2])

        def right_x():
            return right(0)

        def right_t():
            return right(1)

        if k == 0:
            multiply(h, k, ((0, right_x),))
        else:
            multiply(h, k, ((1, right_x), (0 if tiles == 0 else 2, right_t)))

    def sum1(h, k):
        rights[h][k, chunk(r), :] = tall(y_total(h, k)).astype(BF16)

    def dot2(h):
        for m in range(2):
            if (h, m) in Z_TREES:
                for q in (1, 2, 4, 6, 7):
                    piece = rights[h].at[m, chunk(wrap(r - q, N)), :]
                    received(piece, z_rs.at[h, m, q - 1])
        multiply(h, 2, ((1, lambda: rights[h][0]), (0, lambda: rights[h][1])))

    def fin(h):
        lanes = lanes_of(h)
        out_ref[:, lanes] = 1.5 * tm[:, lanes] - 0.5 * y_total(h, 2)

    steps = {
        "prep": prep, "a1": a1, "a1f": a1f, "x": x, "left": left_panel, "z0": z0, "z1": z1, "zt": zt,
        "y": y, "yt": yt, "dot1": dot1, "sum": sum1, "dot2": dot2, "fin": fin,
    }
    for name, *which in ORDER:
        steps[name](*which)

    for m in range(2):
        all_sent(a1_send.at[m, pl.ds(0, N - 1)], a1_ss.at[m])
        all_sent(lt.at[m, pl.ds(0, 7 * PAD), :], x_ss.at[m])
        all_sent(pairs.at[m, pl.ds(0, N - 1)], z0_ss.at[m])
        for h in range(len(CHUNKS)):
            all_sent(rights[h].at[m, pl.ds(0, 7 * PAD), :], z_ss.at[h, m])
    all_sent(ends.at[pl.ds(0, N - 1)], z0_ss.at[2])
    for h in range(len(CHUNKS)):
        all_sent(slots[h], y_ss.at[h])


def body(x_matrix, tangent, fill_x, fill_t):
    count = len(CHUNKS)
    vmem = pltpu.VMEM
    dma = pltpu.SemaphoreType.DMA
    hbm = pl.BlockSpec(memory_space=pl.ANY)
    return pl.pallas_call(
        kernel,
        out_shape=jax.ShapeDtypeStruct((ROWS, WIDTH), F32),
        in_specs=[hbm] * 4,
        out_specs=pl.BlockSpec(memory_space=vmem),
        scratch_shapes=[
            *[vmem(a.shape, a.dtype) for a in (x_matrix, tangent, fill_x, fill_t)],
            vmem((2, N, PAD, 128), BF16),
            vmem((2, N, PAD, 128), BF16),
            vmem((2, N * PAD, LANES), BF16),
            vmem((3, LANES, N * PAD), BF16),
            vmem((ROWS, WIDTH), F32),
            vmem((ROWS, WIDTH), F32),
            vmem((2, N, 2 * ROWS, 256), BF16),
            vmem((N, PAD, 128), BF16),
            *[vmem((2, N * PAD, chunk_width(h)), BF16) for h in range(count)],
            *[vmem((3, N, chunk_rows(h), 128), F32) for h in range(count)],
            *[vmem((3 * 7, chunk_rows(h), 128), F32) for h in range(count)],
            dma((4,)),
            dma((2,)), dma((2,)),
            dma((2,)), dma((2, 3)), dma((2,)),
            dma((3,)), dma((3, 7)),
            dma((count, 2)), dma((count, 2, 7)),
            dma((count,)), dma((count, 3 * 7)),
        ],
        compiler_params=pltpu.CompilerParams(
            collective_id=0, has_side_effects=True, vmem_limit_bytes=60 * 1024 * 1024
        ),
    )(x_matrix, tangent, fill_x, fill_t)


def solution(mesh):
    placed = (P(("row", "depth"), "col"), P(("row", "depth"), "col"), P(), P())
    return jax.shard_map(
        body, mesh=mesh, in_specs=placed, out_specs=P(("row", "depth"), "col"), check_vma=False
    )
```

```python
import jax
import jax.numpy as jnp
from jax import lax
from jax.experimental import pallas as pl
from jax.experimental.pallas import tpu as pltpu
from jax.sharding import PartitionSpec as P

MESH = pl.DeviceIdType.MESH
F32 = jnp.float32
BF16 = jnp.bfloat16
N = 8
NX = 4
ROWS = 72
PAD = 80
WIDTH = 576
LANES = 640
CHUNKS = ((0, 1, 0), (1, 1, 0), (2, 1, 0), (3, 1, 0), (4, 0, 1))
Z_TREES = ((3, 0), (3, 1), (4, 0), (4, 1))
Y_TREES = ((4, 2),)
RING_STEPS = ((4, 3), (3, 4))
SHORT = 2
ORDER = (
    ("prep", 0), ("a1", 0), ("prep", 1), ("z0", 0, 0, 0), ("z0", 1, 1, 0), ("z0", 0, 1, 0), ("z0", 1, 0, 0),
    ("a1", 1), ("z0", 2, 1, 0), ("z0", 2, 0, 0), ("z0", 0, 0, 1), ("z0", 1, 1, 1), ("z0", 0, 1, 1),
    ("z0", 1, 0, 1), ("a1f", 0), ("z0", 2, 1, 1), ("z0", 0, 0, 2), ("z0", 1, 1, 2), ("z0", 0, 1, 2),
    ("z0", 1, 0, 2), ("a1f", 1), ("z0", 2, 1, 2), ("z0", 0, 0, 3), ("z0", 1, 1, 3), ("z0", 0, 1, 3),
    ("z0", 2, 0, 1), ("x", 0, 2), ("z0", 1, 0, 3), ("x", 0, 3), ("x", 0, 1), ("z0", 2, 1, 3), ("left", 0),
    ("z0", 1, 1, 4), ("dot1", 2, 0), ("y", 2, 0, 1, 0), ("y", 2, 0, 0, 0), ("z0", 2, 0, 2), ("dot1", 3, 0),
    ("x", 1, 1), ("z0", 0, 0, 4), ("y", 3, 0, 1, 0), ("x", 1, 2), ("y", 3, 0, 0, 0), ("dot1", 0, 0),
    ("y", 0, 0, 0, 0), ("y", 0, 0, 1, 0), ("x", 1, 3), ("dot1", 1, 0), ("y", 1, 0, 0, 0), ("y", 1, 0, 1, 0),
    ("z0", 2, 0, 3), ("y", 2, 0, 1, 1), ("y", 2, 0, 0, 1), ("left", 1), ("y", 3, 0, 1, 1),
    ("y", 3, 0, 0, 1), ("dot1", 2, 1), ("y", 2, 1, 1, 0), ("y", 2, 1, 0, 0), ("y", 0, 0, 0, 1),
    ("y", 0, 0, 1, 1), ("dot1", 1, 1), ("y", 1, 0, 1, 1), ("y", 1, 0, 0, 1), ("y", 1, 1, 1, 0),
    ("y", 1, 1, 0, 0), ("z0", 2, 0, 4), ("dot1", 0, 1), ("y", 0, 1, 1, 0), ("y", 0, 1, 0, 0),
    ("y", 2, 0, 0, 2), ("y", 3, 0, 1, 2), ("dot1", 3, 1), ("y", 2, 1, 1, 1), ("y", 2, 0, 1, 2),
    ("y", 3, 1, 0, 0), ("y", 3, 0, 0, 2), ("dot1", 4, 1), ("dot1", 4, 0), ("y", 1, 0, 1, 2),
    ("y", 1, 0, 0, 2), ("y", 0, 1, 1, 1), ("y", 1, 1, 0, 1), ("y", 3, 1, 1, 0), ("y", 2, 1, 0, 1),
    ("y", 2, 0, 0, 3), ("y", 3, 0, 1, 3), ("y", 2, 1, 1, 2), ("y", 3, 1, 0, 1), ("y", 0, 0, 0, 2),
    ("y", 0, 1, 0, 1), ("y", 1, 0, 1, 3), ("y", 3, 0, 0, 3), ("y", 1, 0, 0, 3), ("y", 1, 1, 0, 2),
    ("y", 0, 1, 1, 2), ("y", 1, 1, 1, 1), ("y", 3, 1, 1, 1), ("y", 2, 0, 1, 3), ("y", 2, 1, 0, 2),
    ("y", 3, 0, 1, 4), ("y", 2, 0, 0, 4), ("sum", 2, 0), ("z1", 2, 0, 0, 0), ("z1", 2, 0, 1, 0),
    ("sum", 3, 0), ("zt", 3, 0, 0), ("y", 3, 1, 0, 2), ("y", 2, 1, 1, 3), ("y", 0, 0, 1, 2),
    ("y", 0, 0, 0, 3), ("y", 1, 0, 1, 4), ("y", 4, 0, 0, 0), ("y", 4, 1, 1, 0), ("y", 0, 1, 0, 2),
    ("sum", 1, 0), ("z1", 1, 0, 1, 0), ("z1", 1, 0, 0, 0), ("y", 0, 1, 1, 3), ("y", 1, 1, 0, 3),
    ("y", 2, 1, 0, 3), ("y", 1, 1, 1, 2), ("z1", 2, 0, 0, 1), ("y", 3, 1, 1, 2), ("z1", 2, 0, 1, 1),
    ("y", 3, 1, 0, 3), ("y", 2, 1, 1, 4), ("sum", 2, 1), ("z1", 2, 1, 1, 0), ("z1", 2, 1, 0, 0),
    ("y", 0, 0, 0, 4), ("y", 4, 0, 1, 0), ("y", 0, 0, 1, 3), ("sum", 0, 0), ("z1", 0, 0, 0, 0),
    ("y", 4, 0, 0, 1), ("y", 4, 1, 1, 1), ("y", 4, 1, 0, 0), ("z1", 1, 0, 0, 1), ("z1", 0, 0, 1, 0),
    ("z1", 1, 0, 1, 1), ("y", 0, 1, 0, 3), ("zt", 3, 0, 5), ("y", 0, 1, 1, 4), ("sum", 0, 1),
    ("z1", 0, 1, 1, 0), ("z1", 0, 1, 0, 0), ("z1", 2, 0, 0, 2), ("y", 1, 1, 1, 3), ("y", 1, 1, 0, 4),
    ("sum", 1, 1), ("z1", 1, 1, 1, 0), ("z1", 1, 1, 0, 0), ("z1", 2, 1, 1, 1), ("z1", 2, 1, 0, 1),
    ("y", 3, 1, 1, 3), ("y", 3, 1, 0, 4), ("sum", 3, 1), ("zt", 3, 1, 0), ("y", 4, 0, 0, 2),
    ("y", 4, 0, 1, 1), ("z1", 0, 1, 1, 1), ("y", 4, 1, 1, 2), ("z1", 0, 0, 0, 1), ("y", 4, 1, 0, 1),
    ("z1", 1, 0, 0, 2), ("z1", 1, 1, 1, 1), ("z1", 2, 1, 1, 2), ("z1", 1, 1, 0, 1), ("z1", 0, 0, 1, 1),
    ("z1", 2, 0, 1, 2), ("z1", 2, 0, 0, 3), ("z1", 0, 1, 0, 1), ("y", 4, 0, 0, 3), ("zt", 3, 0, 3),
    ("y", 4, 0, 1, 2), ("z1", 2, 1, 0, 2), ("z1", 1, 0, 1, 2), ("z1", 0, 1, 1, 2), ("y", 4, 1, 1, 3),
    ("zt", 3, 1, 5), ("z1", 1, 1, 1, 2), ("y", 4, 1, 0, 2), ("z1", 0, 0, 0, 2), ("zt", 3, 1, 3),
    ("z1", 2, 1, 1, 3), ("y", 4, 0, 0, 4), ("z1", 0, 0, 1, 2), ("z1", 1, 1, 0, 2), ("y", 4, 0, 1, 3),
    ("z1", 1, 0, 0, 3), ("z1", 2, 0, 1, 3), ("sum", 4, 0), ("zt", 4, 0, 0), ("z1", 2, 1, 0, 3),
    ("y", 4, 1, 1, 4), ("y", 4, 1, 0, 3), ("z1", 1, 1, 1, 3), ("z1", 0, 0, 0, 3), ("z1", 2, 0, 0, 4),
    ("sum", 4, 1), ("z1", 0, 1, 0, 2), ("z1", 0, 1, 1, 3), ("zt", 4, 1, 0), ("dot2", 3), ("z1", 2, 1, 1, 4),
    ("dot2", 2), ("y", 2, 2, 0, 0), ("y", 3, 2, 0, 0), ("y", 3, 2, 1, 0), ("z1", 1, 0, 1, 3),
    ("y", 2, 2, 1, 0), ("z1", 1, 1, 0, 3), ("z1", 1, 0, 0, 4), ("z1", 1, 1, 1, 4), ("dot2", 1),
    ("z1", 0, 0, 0, 4), ("zt", 4, 0, 3), ("z1", 0, 0, 1, 3), ("z1", 0, 1, 1, 4), ("zt", 4, 0, 5),
    ("y", 1, 2, 0, 0), ("z1", 0, 1, 0, 3), ("y", 1, 2, 1, 0), ("dot2", 0), ("y", 0, 2, 1, 0),
    ("y", 0, 2, 0, 0), ("y", 3, 2, 1, 1), ("y", 2, 2, 0, 1), ("zt", 4, 1, 5), ("y", 3, 2, 0, 1),
    ("zt", 4, 1, 3), ("y", 2, 2, 1, 1), ("y", 1, 2, 1, 1), ("y", 1, 2, 0, 1), ("y", 0, 2, 0, 1),
    ("y", 0, 2, 1, 1), ("y", 2, 2, 0, 2), ("y", 3, 2, 1, 2), ("dot2", 4), ("yt", 4, 2, 0),
    ("y", 1, 2, 1, 2), ("y", 1, 2, 0, 2), ("y", 2, 2, 1, 2), ("y", 0, 2, 0, 2), ("y", 3, 2, 0, 2),
    ("y", 3, 2, 1, 3), ("yt", 4, 2, 1), ("yt", 4, 2, 2), ("y", 1, 2, 1, 3), ("y", 0, 2, 1, 2),
    ("y", 2, 2, 0, 3), ("y", 2, 2, 1, 3), ("y", 0, 2, 0, 3), ("y", 3, 2, 0, 3), ("y", 3, 2, 1, 4),
    ("y", 1, 2, 0, 3), ("y", 2, 2, 0, 4), ("y", 1, 2, 1, 4), ("fin", 1), ("fin", 3), ("fin", 2), ("fin", 4),
    ("y", 0, 2, 1, 3), ("y", 0, 2, 0, 4), ("fin", 0),
)


def chunk_width(h):
    _, tiles, fold = CHUNKS[h]
    return tiles * 128 + fold * 64


def chunk_rows(h):
    _, tiles, fold = CHUNKS[h]
    return tiles * ROWS + fold * 40


def pack(value, h):
    _, tiles, fold = CHUNKS[h]
    rows = [value[:, t * 128 : (t + 1) * 128] for t in range(tiles)]
    if fold:
        last = value[:, tiles * 128 :]
        low = jnp.concatenate([last[40:], jnp.zeros((8, 64), F32)], axis=0)
        rows.append(jnp.concatenate([last[:40], low], axis=1))
    return rows[0] if len(rows) == 1 else jnp.concatenate(rows, axis=0)


def unpack(value, h):
    _, tiles, fold = CHUNKS[h]
    columns = [value[t * ROWS : (t + 1) * ROWS] for t in range(tiles)]
    if fold:
        last = value[tiles * ROWS :]
        columns.append(jnp.concatenate([last[:, :64], last[:32, 64:]], axis=0))
    return columns[0] if len(columns) == 1 else jnp.concatenate(columns, axis=1)


def kernel(x_hbm, t_hbm, fx_hbm, ft_hbm, out_ref, *scratch):
    scratch = list(scratch)
    ins = [scratch.pop(0) for _ in range(4)]
    a1_send, a1_recv, lt, left, xm, tm, pairs, ends = [scratch.pop(0) for _ in range(8)]
    rights = [scratch.pop(0) for _ in CHUNKS]
    parts = [scratch.pop(0) for _ in CHUNKS]
    slots = [scratch.pop(0) for _ in CHUNKS]
    shorts = [scratch.pop(0) for _ in CHUNKS]
    in_s, a1_ss, a1_rs, x_ss, x_rs, c_rs, z0_ss, z0_rs, z_ss, z_rs, y_ss, y_rs, b_ss = scratch

    r = lax.axis_index("row")
    c = lax.axis_index("col")
    d = lax.axis_index("depth")
    chip = c // 2
    core = lax.rem(c, 2)

    def wrap(value, size):
        return lax.rem(value + 2 * size, size)

    def at_row(step):
        return (wrap(r + step, N), c, d)

    def at_depth(step):
        return (r, c, wrap(d + step, N))

    def at_chip(step):
        return (r, wrap(chip + step, NX) * 2 + core, d)

    partner = (r, chip * 2 + 1 - core, d)

    barrier = pltpu.get_barrier_semaphore()
    greeted = [at_depth(s) for s in (4, 3, 5, 2, 6, 1, 7)]
    greeted += [at_row(s) for s in ((1, -1, 3, -3) if Z_TREES else (1, -1))]
    greeted += [at_chip(1), at_chip(2), at_chip(3), partner]
    for device in greeted:
        pl.semaphore_signal(barrier, inc=1, device_id=device, device_id_type=MESH)

    fetches = [
        pltpu.make_async_copy(src, dst, in_s.at[k])
        for k, (src, dst) in enumerate(zip((x_hbm, t_hbm, fx_hbm, ft_hbm), ins))
    ]
    for k in (0, 2, 1, 3):
        fetches[k].start()

    row_start = (r * N + d) * ROWS
    col_start = c * WIDTH

    def expand(fill):
        count = fill.shape[0]
        row_ids = (row_start + lax.broadcasted_iota(jnp.int32, (ROWS, count), 0)) >> 7
        row_hot = (row_ids == lax.broadcasted_iota(jnp.int32, (ROWS, count), 1)).astype(F32)
        col_ids = (col_start + lax.broadcasted_iota(jnp.int32, (count, WIDTH), 1)) >> 7
        col_hot = (col_ids == lax.broadcasted_iota(jnp.int32, (count, WIDTH), 0)).astype(F32)
        inner = jnp.dot(row_hot, fill.astype(F32), preferred_element_type=F32)
        return jnp.dot(inner, col_hot, preferred_element_type=F32)

    def chunk(index):
        return pl.ds(pl.multiple_of(index * PAD, 16), PAD)

    def tall(value):
        return jnp.concatenate([value, jnp.zeros((PAD - ROWS, value.shape[1]), F32)], axis=0)

    def copy(src, dst, send_sem, recv_sem, device):
        return pltpu.make_async_remote_copy(
            src_ref=src, dst_ref=dst, send_sem=send_sem, recv_sem=recv_sem,
            device_id=device, device_id_type=MESH,
        )

    def send(src, dst, send_sem, recv_sem, device):
        copy(src, dst, send_sem, recv_sem, device).start()

    def received(piece, recv_sem):
        copy(piece, piece, recv_sem, recv_sem, partner).wait_recv()

    def all_sent(pieces, send_sem):
        copy(pieces, pieces, send_sem, send_sem, partner).wait_send()

    def prep(m):
        fetches[m].wait()
        fetches[2 + m].wait()
        masked = ins[m][...].astype(F32) * expand(ins[2 + m][...])
        (xm, tm)[m][...] = masked
        padded = tall(masked)
        for j in range(N):
            piece = padded[:, j * ROWS : (j + 1) * ROWS]
            wide = jnp.concatenate([piece, jnp.zeros((PAD, 128 - ROWS), F32)], axis=1)
            a1_send[m, j] = wide.astype(BF16)
        if m == 1:
            both = jnp.concatenate([xm[...], masked], axis=0)
            for u in range(2):
                pairs[u, r] = both[:, u * 256 : (u + 1) * 256].astype(BF16)
            last = jnp.concatenate([both[:ROWS, 512:], both[ROWS:, 512:]], axis=1)
            ends[r] = tall(last).astype(BF16)
        a1_recv[m, d] = a1_send[m, d]
        if m == 0:
            pl.semaphore_wait(barrier, len(greeted))

    def a1(m):
        for s in (4, 3, 5, 2, 6, 1, 7):
            to = wrap(d + s, N)
            send(a1_send.at[m, to], a1_recv.at[m, d], a1_ss.at[m], a1_rs.at[m], (r, c, to))

    def lt_piece(m, owner_chip, owner_core):
        return lt.at[m, chunk(wrap(owner_chip, NX) * 2 + owner_core), :]

    def a1f(m):
        received(a1_recv.at[m, pl.ds(0, N - 1)], a1_rs.at[m])
        stacked = a1_recv[m].astype(F32)[:, :ROWS, :].reshape(N * ROWS, 128)
        turned = tall(jnp.transpose(stacked)[:ROWS])
        turned = jnp.concatenate([turned, jnp.zeros((PAD, LANES - WIDTH), F32)], axis=1)
        lt[m, chunk(c), :] = turned.astype(BF16)
        piece = lt_piece(m, chip, core)
        for q in (2, 1, 3):
            send(piece, piece, x_ss.at[m], x_rs.at[m, q - 1], at_chip(q))
        send(piece, piece, x_ss.at[m], c_rs.at[m], partner)

    def x(m, q):
        piece = lt_piece(m, chip - q, core)
        received(piece, x_rs.at[m, q - 1])
        send(piece, piece, x_ss.at[m], c_rs.at[m], partner)

    def left_panel(m):
        received(lt.at[m, pl.ds(0, NX * PAD), :], c_rs.at[m])
        for i in range(LANES // 128):
            lanes = slice(i * 128, (i + 1) * 128)
            panel = lt[m, :, lanes].astype(F32)
            left[m, lanes, :] = jnp.transpose(panel).astype(BF16)
            if m == 0:
                split = panel.reshape(N, PAD, 128)
                moved = jnp.concatenate([split[:, ROWS:], split[:, :ROWS]], axis=1)
                left[2, lanes, :] = jnp.transpose(moved.reshape(N * PAD, 128)).astype(BF16)

    def ring(piece_of, send_sem, recv_sems, m, e, s):
        sign, steps = (1, -1)[e], RING_STEPS[m][e]
        at = e * RING_STEPS[m][0]
        piece = piece_of(wrap(r - sign * s, N))
        if s > 0:
            received(piece, recv_sems.at[at + s - 1])
        if s < steps:
            send(piece, piece, send_sem, recv_sems.at[at + s], at_row(sign))

    def z0(u, e, s):
        def piece_of(index):
            return ends.at[index] if u == 2 else pairs.at[u, index]

        ring(piece_of, z0_ss.at[u], z0_rs.at[u], u % 2, e, s)

    def z1(h, m, e, s):
        def piece_of(index):
            return rights[h].at[m, chunk(index), :]

        ring(piece_of, z_ss.at[h, m], z_rs.at[h, m], m, e, s)

    def zt(h, m, q):
        piece = rights[h].at[m, chunk(wrap(r - q, N)), :]
        if q > 0:
            received(piece, z_rs.at[h, m, q - 1])
        for step in {0: (3, -3, 1, -1), 3: (1, -1), 5: (1,)}[q]:
            there = (q + step) % N
            send(piece, piece, z_ss.at[h, m], z_rs.at[h, m, there - 1], at_row(step))

    def y(h, k, e, s):
        sign, (plus, minus) = (1, -1)[e], RING_STEPS[(k + h) % 2]
        steps = (plus, minus)[e]
        part, slot, at = parts[h], slots[h], 7 * k + e * plus
        dest = wrap(d + sign * (steps - s), N)
        short = SHORT if k == 1 else 0
        came = None
        if s > 0:
            piece = shorts[h].at[1, e, s - 1] if s <= short else slot.at[at + s - 1]
            received(piece, y_rs.at[h, at + s - 1])
            if s < steps:
                came = piece[...].astype(F32) + part[k, dest]
        if s == steps:
            return
        if s < short:
            value = part[k, dest] if came is None else came
            shorts[h][0, e, s] = value.astype(BF16)
            source, target, done = shorts[h].at[0, e, s], shorts[h].at[1, e, s], b_ss.at[h]
        else:
            source, target, done = part.at[k, dest], slot.at[at + s], y_ss.at[h]
            if came is not None:
                slot[at + s - 1] = came
                source = slot.at[at + s - 1]
        send(source, target, done, y_rs.at[h, at + s], at_depth(sign))

    def yt(h, k, stage):
        part, slot, at = parts[h], slots[h], 7 * k

        def go(source, index, step):
            send(source, slot.at[at + index], y_ss.at[h], y_rs.at[h, at + index], at_depth(step))

        def mine(step):
            return wrap(d + step, N)

        if stage == 0:
            for index, (away, step) in enumerate(((4, 1), (2, -1), (-2, 1), (1, 1), (-1, -1))):
                go(part.at[k, mine(away)], index, step)
        elif stage == 1:
            for index in (0, 1):
                received(slot.at[at + index], y_rs.at[h, at + index])
            slot[at] = slot[at] + slot[at + 1] + part[k, mine(3)]
            go(slot.at[at], 5, 3)
        else:
            received(slot.at[at + 2], y_rs.at[h, at + 2])
            slot[at + 2] = slot[at + 2] + part[k, mine(-3)]
            go(slot.at[at + 2], 6, -3)

    def y_total(h, k):
        at = 7 * k
        if (h, k) in Y_TREES:
            last = (3, 4, 5, 6)
            for index in last:
                received(slots[h].at[at + index], y_rs.at[h, at + index])
        else:
            last = (RING_STEPS[(k + h) % 2][0] - 1, 6)
        total = parts[h][k, d]
        for index in last:
            total = total + slots[h][at + index]
        return unpack(total, h)

    def multiply(h, k, terms):
        blocks = 4
        tile = blocks * ROWS

        def one(i, carry):
            rows = pl.ds(pl.multiple_of(i * tile, 16), tile)
            total = None
            for m, right in terms:
                term = jnp.dot(left[m, rows, :], right(), preferred_element_type=F32)
                total = term if total is None else total + term
            for b in range(blocks):
                parts[h][k, i * blocks + b] = pack(total[b * ROWS : (b + 1) * ROWS], h)
            return carry

        lax.fori_loop(0, N // blocks, one, 0)

    def lanes_of(h):
        start = CHUNKS[h][0] * 128
        return slice(start, start + chunk_width(h))

    def dot1(h, k):
        tile, tiles, _ = CHUNKS[h]

        def right(m):
            if tiles == 0:
                value = ends[:, :, m * 64 : (m + 1) * 64]
            else:
                at = (tile % 2) * 128
                value = pairs[tile // 2, :, m * 64 : m * 64 + PAD, at : at + 128]
            return value.reshape(N * PAD, value.shape[2])

        def right_x():
            return right(0)

        def right_t():
            return right(1)

        if k == 0:
            multiply(h, k, ((0, right_x),))
        else:
            multiply(h, k, ((1, right_x), (0 if tiles == 0 else 2, right_t)))

    def sum1(h, k):
        rights[h][k, chunk(r), :] = tall(y_total(h, k)).astype(BF16)

    def dot2(h):
        for m in range(2):
            if (h, m) in Z_TREES:
                for q in (1, 2, 4, 6, 7):
                    piece = rights[h].at[m, chunk(wrap(r - q, N)), :]
                    received(piece, z_rs.at[h, m, q - 1])
        multiply(h, 2, ((1, lambda: rights[h][0]), (0, lambda: rights[h][1])))

    def fin(h):
        lanes = lanes_of(h)
        out_ref[:, lanes] = 1.5 * tm[:, lanes] - 0.5 * y_total(h, 2)

    steps = {
        "prep": prep, "a1": a1, "a1f": a1f, "x": x, "left": left_panel, "z0": z0, "z1": z1, "zt": zt,
        "y": y, "yt": yt, "dot1": dot1, "sum": sum1, "dot2": dot2, "fin": fin,
    }
    for name, *which in ORDER:
        steps[name](*which)

    for m in range(2):
        all_sent(a1_send.at[m, pl.ds(0, N - 1)], a1_ss.at[m])
        all_sent(lt.at[m, pl.ds(0, 7 * PAD), :], x_ss.at[m])
        all_sent(pairs.at[m, pl.ds(0, N - 1)], z0_ss.at[m])
        for h in range(len(CHUNKS)):
            all_sent(rights[h].at[m, pl.ds(0, 7 * PAD), :], z_ss.at[h, m])
    all_sent(ends.at[pl.ds(0, N - 1)], z0_ss.at[2])
    for h in range(len(CHUNKS)):
        all_sent(slots[h].at[pl.ds(0, 3 * 7 - 2 * SHORT)], y_ss.at[h])
        all_sent(shorts[h].at[0], b_ss.at[h])


def body(x_matrix, tangent, fill_x, fill_t):
    count = len(CHUNKS)
    vmem = pltpu.VMEM
    dma = pltpu.SemaphoreType.DMA
    hbm = pl.BlockSpec(memory_space=pl.ANY)
    return pl.pallas_call(
        kernel,
        out_shape=jax.ShapeDtypeStruct((ROWS, WIDTH), F32),
        in_specs=[hbm] * 4,
        out_specs=pl.BlockSpec(memory_space=vmem),
        scratch_shapes=[
            *[vmem(a.shape, a.dtype) for a in (x_matrix, tangent, fill_x, fill_t)],
            vmem((2, N, PAD, 128), BF16),
            vmem((2, N, PAD, 128), BF16),
            vmem((2, N * PAD, LANES), BF16),
            vmem((3, LANES, N * PAD), BF16),
            vmem((ROWS, WIDTH), F32),
            vmem((ROWS, WIDTH), F32),
            vmem((2, N, 2 * ROWS, 256), BF16),
            vmem((N, PAD, 128), BF16),
            *[vmem((2, N * PAD, chunk_width(h)), BF16) for h in range(count)],
            *[vmem((3, N, chunk_rows(h), 128), F32) for h in range(count)],
            *[vmem((3 * 7, chunk_rows(h), 128), F32) for h in range(count)],
            *[vmem((2, 2, SHORT, chunk_rows(h), 128), BF16) for h in range(count)],
            dma((4,)),
            dma((2,)), dma((2,)),
            dma((2,)), dma((2, 3)), dma((2,)),
            dma((3,)), dma((3, 7)),
            dma((count, 2)), dma((count, 2, 7)),
            dma((count,)), dma((count, 3 * 7)), dma((count,)),
        ],
        compiler_params=pltpu.CompilerParams(
            collective_id=0, has_side_effects=True, vmem_limit_bytes=60 * 1024 * 1024
        ),
    )(x_matrix, tangent, fill_x, fill_t)


def solution(mesh):
    placed = (P(("row", "depth"), "col"), P(("row", "depth"), "col"), P(), P())
    return jax.shard_map(
        body, mesh=mesh, in_specs=placed, out_specs=P(("row", "depth"), "col"), check_vma=False
    )
```
